256 devices in a mesh: section: 4 (over x), seq: 64 (over z, y, core).
Axes of the slice: x: 4, y: 4, z: 8, core: 2. Of those that a mesh axis runs over, the one named last changes fastest.
Arguments:
- queries: bfloat16 [4, 16384, 2048], P('section', 'seq'), may hold values from -24 to 24
- keys: bfloat16 [4, 16384, 1024], P('section', 'seq'), may hold values from -24 to 24
- values: bfloat16 [4, 16384, 1024], P('section', 'seq'), may hold values from -6 to 6
- segment_ids: int32 [16384], P('seq'), may hold values from 0 to 7, as said below
- positions: int32 [16384], P('seq'), may hold values from 0 to 8191, as said below
- residual_in: bfloat16 [16384, 2048], P('seq'), may hold values from -6 to 6
- post_gain: float32 [4, 2048], P('section'), may hold values from 0.1 to 1.9
Outputs:
- layer_out: bfloat16 [4, 16384, 2048], P('section', 'seq')
The draws below stay inside these ranges and needn't reach their ends.
Inputs may be any that keep to these rules, and one draw needn't show every extreme that they name: `segment_ids`: never falling; each document holds 1 to 8192 tokens, one exactly 8192. `positions`: the token's index minus the index of the first token of its document.
All inputs are finite; a program needn't handle non-finite values.
Results may differ from the reference program's by a relative error of at most 0.011.
Values may be sent and summed in bfloat16 or wider, within the bound.
No kernel may reach another device: no remote copies, remote signals or barrier semaphores. Data moves between devices by JAX's collectives and lax.ppermute only.
A program may use at most 128 MiB of HBM per device.

```python
import math
import jax
import jax.numpy as jnp
from jax import lax

HQ = 8
HK = 4
HD = 256
WINDOW = 4096
TOK_DEV = 256
LAYERS = 4
TOKENS = 16384
DOC_LIMIT = 8192
DOCS = 8


def lifted_heads(key, heads):
    base_key, lift_key = jax.random.split(key)
    base = jax.random.truncated_normal(base_key, -6.0, 6.0, (LAYERS, TOKENS, heads, HD), jnp.float32)
    lift = jnp.exp(jax.random.uniform(lift_key, (LAYERS, TOKENS, heads, 1), jnp.float32, 0.0, math.log(4.0)))
    return (base * lift).reshape(LAYERS, TOKENS, heads * HD).astype(jnp.bfloat16)


def draw_queries(key, part):
    return lifted_heads(jax.random.fold_in(key, 101), HQ)


def draw_keys(key, part):
    return lifted_heads(jax.random.fold_in(key, 202), HK)


def document_layout(key):
    shared = jax.random.fold_in(key, 303)
    place_key, shift_key = jax.random.split(shared)
    others = DOCS - 1
    rest = TOKENS - DOC_LIMIT
    base = rest // others
    reach = max(base // 4, 0)
    shifts = jax.random.randint(shift_key, (others,), -reach, reach + 1).astype(jnp.int32)
    lengths_other = base + shifts - jnp.roll(shifts, 1)
    lengths_other = lengths_other.at[others - 1].add(rest - base * others)
    place = jax.random.randint(place_key, (), 0, DOCS).astype(jnp.int32)
    slot = jnp.arange(DOCS, dtype=jnp.int32)
    before = lengths_other[jnp.clip(slot, 0, others - 1)]
    after = lengths_other[jnp.clip(slot - 1, 0, others - 1)]
    lengths = jnp.where(slot < place, before, jnp.where(slot == place, DOC_LIMIT, after)).astype(jnp.int32)
    ends = jnp.cumsum(lengths).astype(jnp.int32)
    starts = ends - lengths
    token = jnp.arange(TOKENS, dtype=jnp.int32)
    seg = jnp.sum((token[:, None] >= ends[None, :]).astype(jnp.int32), axis=1).astype(jnp.int32)
    hit = (seg[:, None] == slot[None, :]).astype(jnp.int32)
    first = jnp.sum(hit * starts[None, :], axis=1).astype(jnp.int32)
    return (seg, token - first)


def draw_segment_ids(key, part):
    return document_layout(key)[0]


def draw_positions(key, part):
    return document_layout(key)[1]


def level_of(key, dims, cuts, low, top_value):
    level = 1.0
    for dim, shards_of in cuts:
        heights = jax.random.uniform(jax.random.fold_in(jax.random.fold_in(key, 6), dim), (shards_of,), jnp.float32, low / len(cuts), top_value / len(cuts))
        level = level * jnp.repeat(jnp.exp(heights), dims[dim] // shards_of).reshape((-1,) + (1,) * (len(dims) - 1 - dim))
    return level


def centred(rng, extent, width, bound, cuts=(), kind=jnp.bfloat16):
    drawn = width * jax.random.normal(rng, extent, jnp.float32)
    if cuts:
        drawn = drawn * level_of(rng, extent, cuts, -0.22, 0.18)
    return jnp.clip(drawn, -bound, bound).astype(kind)


def setup_inputs(seed: int = 0) -> dict:
    key_of = jax.random.split(jax.random.key(seed), 8)
    queries = draw_queries(jax.random.fold_in(key_of[7], 71), 0)
    keys = draw_keys(jax.random.fold_in(key_of[7], 71), 0)
    values = centred(key_of[2], (LAYERS, TOKENS, HK * HD), 1.0, 6.0, ((0, 4), (1, 64)))
    segment_ids = draw_segment_ids(jax.random.fold_in(key_of[7], 71), 0)
    positions = draw_positions(jax.random.fold_in(key_of[7], 71), 0)
    residual_in = centred(key_of[5], (TOKENS, HQ * HD), 1.0, 6.0, ((0, 64),))
    post_gain = jnp.clip(1.0 + 0.18 * jax.random.normal(key_of[6], (LAYERS, HQ * HD), jnp.float32), 0.1, 1.9)
    return dict(queries=queries, keys=keys, values=values, segment_ids=segment_ids, positions=positions, residual_in=residual_in, post_gain=post_gain)


def rotate(x, position, heads):
    count = x.shape[0]
    half = HD // 2
    parts = x.astype(jnp.float32).reshape(count, heads, HD)
    inverse = jnp.exp(-math.log(10000.0) * jnp.arange(half).astype(jnp.float32) / half)
    angle = position.astype(jnp.float32)[:, None] * inverse[None, :]
    cosine = jnp.cos(angle)[:, None, :]
    sine = jnp.sin(angle)[:, None, :]
    first = parts[:, :, :half]
    second = parts[:, :, half:]
    turned = jnp.concatenate([first * cosine - second * sine, second * cosine + first * sine], axis=-1)
    return turned.reshape(count, heads * HD).astype(jnp.bfloat16)

def one_layer(query_rot, key_rot, value_layer, segment_ids, gain):
    group = HQ // HK
    key_pad = jnp.concatenate([jnp.zeros((WINDOW, HK * HD), jnp.bfloat16), key_rot], axis=0)
    value_pad = jnp.concatenate([jnp.zeros((WINDOW, HK * HD), jnp.bfloat16), value_layer], axis=0)
    seg_pad = jnp.concatenate([jnp.full((WINDOW,), -1, jnp.int32), segment_ids.astype(jnp.int32)], axis=0)
    span = WINDOW + TOK_DEV
    scale = HD ** (-0.5)

    def block(index):
        first = (index * TOK_DEV).astype(jnp.int32)
        query_blk = lax.dynamic_slice_in_dim(query_rot, first, TOK_DEV, 0).astype(jnp.float32)
        query_blk = query_blk.reshape(TOK_DEV, HK, group, HD)
        key_blk = lax.dynamic_slice_in_dim(key_pad, first, span, 0).astype(jnp.float32).reshape(span, HK, HD)
        value_blk = lax.dynamic_slice_in_dim(value_pad, first, span, 0).astype(jnp.float32).reshape(span, HK, HD)
        seg_key = lax.dynamic_slice_in_dim(seg_pad, first, span, 0)
        seg_query = lax.dynamic_slice_in_dim(segment_ids.astype(jnp.int32), first, TOK_DEV, 0)
        query_pos = first + jnp.arange(TOK_DEV).astype(jnp.int32)
        key_pos = first - WINDOW + jnp.arange(span).astype(jnp.int32)
        gap = query_pos[:, None] - key_pos[None, :]
        allowed = (key_pos[None, :] >= 0) & (gap >= 0) & (gap < WINDOW) & (seg_query[:, None] == seg_key[None, :])
        score = jnp.einsum('qgjd,kgd->qgjk', query_blk, key_blk) * scale
        score = 50.0 * jnp.tanh(score / 50.0)
        weight = jnp.where(allowed[:, None, None, :], jnp.exp(score), 0.0)
        total = lax.optimization_barrier(jnp.sum(weight, axis=-1))
        weight_b = weight.astype(jnp.bfloat16).astype(jnp.float32)
        summed = jnp.einsum('qgjk,kgd->qgjd', weight_b, value_blk)
        attended = (summed / total[..., None]).reshape(TOK_DEV, HQ * HD)
        norm = lax.rsqrt(lax.optimization_barrier(jnp.mean(attended * attended, axis=-1, keepdims=True)) + 1e-06)
        return attended * norm * gain[None, :]
    deltas = lax.map(block, jnp.arange(TOKENS // TOK_DEV).astype(jnp.int32))
    return deltas.reshape(TOKENS, HQ * HD)

def reference(queries, keys, values, segment_ids, positions, residual_in, post_gain):
    seg = segment_ids.astype(jnp.int32)
    position = positions.astype(jnp.int32)
    outputs = []
    running = residual_in.astype(jnp.float32)
    for layer in range(LAYERS):
        query_rot = rotate(queries[layer], position, HQ)
        key_rot = rotate(keys[layer], position, HK)
        delta = one_layer(query_rot, key_rot, values[layer], seg, post_gain[layer].astype(jnp.float32))
        running = running + delta
        outputs.append(running.astype(jnp.bfloat16))
    return jnp.stack(outputs, axis=0)
```

```python
import functools
import math

import jax
import jax.numpy as jnp
from jax import lax
from jax.experimental import pallas as pl
from jax.experimental.pallas import tpu as pltpu
from jax.sharding import PartitionSpec as P

HQ = 8
HK = 4
HD = 256
WINDOW = 4096
ROWS = 256
PLANE = 2048
LAYERS = 4
HALF = HD // 2
VMEM = pltpu.VMEM
SMEM = pltpu.SMEM

SHARED_Y = [[z * 8 + y * 2 + c for y in range(4)] for z in range(8) for c in range(2)]
SHARED_XY = [
    [x * 64 + z * 8 + y * 2 + c for x in range(4) for y in range(4)]
    for z in range(8)
    for c in range(2)
]
NEXT_PLANE = [(i, i + 8) for i in range(56)]
OTHER_CORE = [(i, i ^ 1) for i in range(64)]


def vspec():
    return pl.BlockSpec(memory_space=VMEM)


def sspec():
    return pl.BlockSpec(memory_space=SMEM)


def turned(x, cosine, sine):
    first = x[:, :HALF].astype(jnp.float32)
    second = x[:, HALF:].astype(jnp.float32)
    return (
        (first * cosine - second * sine).astype(jnp.bfloat16),
        (second * cosine + first * sine).astype(jnp.bfloat16),
    )


def rotate_kv_kernel(cos_ref, sin_ref, k_ref, v_ref, km_ref, vm_ref):
    for h in range(HK):
        a, b = turned(k_ref[:, h * HD : (h + 1) * HD], cos_ref[...], sin_ref[...])
        km_ref[h, :, :HALF] = a
        km_ref[h, :, HALF:] = b
        vm_ref[h] = v_ref[:, h * HD : (h + 1) * HD]


def rotate_q_kernel(cos_ref, sin_ref, q_ref, qm_ref):
    for h in range(HQ):
        a, b = turned(q_ref[:, h * HD : (h + 1) * HD], cos_ref[...], sin_ref[...])
        rows = pl.ds((h % 2) * ROWS, ROWS)
        qm_ref[h // 2, rows, :HALF] = a
        qm_ref[h // 2, rows, HALF:] = b


def attend_kernel(back, first, last, meta_ref, lo_ref, q_ref, *refs):
    k_own, k_oth, v_own, v_oth = refs[:4]
    if first:
        num, den = refs[4:]
    elif last:
        num_in, den_in, out_ref, num, den = refs[4:]
    else:
        num_in, den_in, num, den = refs[4:]
    if first:
        num[...] = jnp.zeros_like(num)
        den[...] = jnp.zeros_like(den)
    else:
        num[...] = num_in[...]
        den[...] = den_in[...]
    plane0 = meta_ref[0]
    core = meta_ref[1]
    keys0 = plane0 - back * PLANE

    def unit(r, j, masked):
        query = q_ref[r]
        q_base = plane0 + r * 512 + core * ROWS
        total = None
        added = None
        for k_ref, v_ref, side in ((k_own, v_own, core), (k_oth, v_oth, 1 - core)):
            score = lax.dot_general(
                query,
                k_ref[j],
                (((1,), (1,)), ((), ())),
                preferred_element_type=jnp.float32,
            )
            weight = jnp.exp2(jnp.tanh(score * (1.0 / 800.0)) * (50.0 / math.log(2.0)))
            if masked:
                base = keys0 + j * 512 + side * ROWS
                key = base + lax.broadcasted_iota(jnp.int32, (512, ROWS), 1)
                row = q_base + (lax.broadcasted_iota(jnp.int32, (512, ROWS), 0) & (ROWS - 1))
                ok = (key >= lo_ref[r]) & (key <= row)
                weight = jnp.where(ok, weight, 0.0)
            lanes = weight[:, :HALF] + weight[:, HALF:]
            part = jnp.dot(
                weight.astype(jnp.bfloat16), v_ref[j], preferred_element_type=jnp.float32
            )
            total = lanes if total is None else total + lanes
            added = part if added is None else added + part
        num[r] += added
        den[r] += total

    def step(i, carry):
        r = i // 4
        j = lax.rem(i, 4)
        q_base = plane0 + r * 512 + core * ROWS
        base = keys0 + j * 512
        live = (base + 511 >= meta_ref[2 + r]) & (base <= q_base + ROWS - 1)
        clear = (base >= meta_ref[6 + r]) & (base + 511 <= q_base)

        @pl.when(live & clear)
        def _():
            unit(r, j, False)

        @pl.when(live & jnp.logical_not(clear))
        def _():
            unit(r, j, True)

        return carry

    lax.fori_loop(0, 16, step, 0)
    if last:
        for k in range(4):
            whole = num[k] / jnp.sum(den[k], axis=-1, keepdims=True)
            whole = whole.astype(jnp.bfloat16)
            for q in range(4):
                for h in range(2):
                    out_ref[q * 4 + k, :, h * HD : (h + 1) * HD] = whole[
                        h * ROWS + q * 64 : h * ROWS + q * 64 + 64
                    ]


def attend(back, first, last, meta, lo_rows, query, k_own, k_oth, v_own, v_oth, num, den):
    sums = [
        jax.ShapeDtypeStruct((4, 512, HD), jnp.float32),
        jax.ShapeDtypeStruct((4, 512, HALF), jnp.float32),
    ]
    args = [meta, lo_rows, query, k_own, k_oth, v_own, v_oth]
    if not first:
        args += [num, den]
    scratch = []
    if last:
        outs = jax.ShapeDtypeStruct((16, 64, 512), jnp.bfloat16)
        scratch = [VMEM((4, 512, HD), jnp.float32), VMEM((4, 512, HALF), jnp.float32)]
        out_specs = vspec()
    else:
        outs = sums
        out_specs = [vspec(), vspec()]
    pairs = {0: 20, 1: 32, 2: 20}[back]
    return pl.pallas_call(
        functools.partial(attend_kernel, back, first, last),
        out_shape=outs,
        in_specs=[sspec()] + [vspec()] * (len(args) - 1),
        out_specs=out_specs,
        scratch_shapes=scratch,
        compiler_params=pltpu.CompilerParams(vmem_limit_bytes=48 << 20),
        cost_estimate=pl.CostEstimate(
            flops=pairs * 512 * 256 * 256 * 4,
            bytes_accessed=8 << 20,
            transcendentals=pairs * 512 * 256 * 2,
        ),
        name="attend_%d" % back,
    )(*args)


def combine_kernel(meta_ref, got_ref, res_ref, gain_ref, out_ref):
    rows = pl.ds(pl.multiple_of(meta_ref[0] * 64, 64), 64)
    running = res_ref[rows, :].astype(jnp.float32)
    running = [running[:, h * 512 : (h + 1) * 512] for h in range(4)]
    for layer in range(LAYERS):
        parts = [got_ref[layer * 4 + h].astype(jnp.float32) for h in range(4)]
        square = sum(jnp.sum(p * p, axis=-1, keepdims=True) for p in parts)
        norm = lax.rsqrt(square * (1.0 / (HQ * HD)) + 1e-06)
        for h in range(4):
            gain = gain_ref[layer : layer + 1, h * 512 : (h + 1) * 512]
            running[h] = running[h] + parts[h] * norm * gain
            out_ref[layer, :, h * 512 : (h + 1) * 512] = running[h].astype(jnp.bfloat16)


def per_device(queries, keys, values, segment_ids, positions, residual_in, post_gain):
    device = lax.axis_index("seq")
    section = lax.axis_index("section").astype(jnp.int32)
    plane0 = (device // 8 * PLANE).astype(jnp.int32)
    core = (device % 2).astype(jnp.int32)

    inverse = jnp.exp(-math.log(10000.0) * jnp.arange(HALF).astype(jnp.float32) / HALF)
    angle = positions.astype(jnp.float32)[:, None] * inverse[None, :]
    cosine = jnp.cos(angle)
    sine = jnp.sin(angle)

    gains = lax.all_gather(post_gain, "section", tiled=True)
    places = lax.all_gather(positions, "seq", axis_index_groups=SHARED_Y)

    k_msg, v_msg = pl.pallas_call(
        rotate_kv_kernel,
        out_shape=[jax.ShapeDtypeStruct((HK, ROWS, HD), jnp.bfloat16)] * 2,
        in_specs=[vspec()] * 4,
        out_specs=[vspec()] * 2,
        name="rotate_kv",
    )(cosine, sine, keys[0], values[0])
    q_msg = pl.pallas_call(
        rotate_q_kernel,
        out_shape=jax.ShapeDtypeStruct((HK, 2 * ROWS, HD), jnp.bfloat16),
        in_specs=[vspec()] * 3,
        out_specs=vspec(),
        name="rotate_q",
    )(cosine, sine, queries[0])

    def over_y(x):
        return lax.all_to_all(x, "seq", 0, 0, axis_index_groups=SHARED_Y)

    def onward(x):
        return lax.ppermute(x, "seq", NEXT_PLANE)

    def other(x):
        return lax.ppermute(x, "seq", OTHER_CORE)

    k0 = over_y(k_msg)
    v0 = over_y(v_msg)
    query = over_y(q_msg)
    k1 = onward(k0)
    v1 = onward(v0)
    k2 = onward(k1)
    v2 = onward(v1)

    token = (
        plane0
        + core * ROWS
        + jnp.arange(4, dtype=jnp.int32)[:, None] * 512
        + jnp.arange(ROWS, dtype=jnp.int32)[None, :]
    )
    lo = token - jnp.minimum(places, WINDOW - 1)
    meta = jnp.concatenate([jnp.stack([plane0, core]), lo[:, 0], lo[:, ROWS - 1]])
    lo_rows = jnp.concatenate([lo, lo], axis=1)[:, :, None]

    num, den = attend(
        0, True, False, meta, lo_rows, query, k0, other(k0), v0, other(v0), None, None
    )
    num, den = attend(
        1, False, False, meta, lo_rows, query, k1, other(k1), v1, other(v1), num, den
    )
    sent = attend(2, False, True, meta, lo_rows, query, k2, other(k2), v2, other(v2), num, den)
    got = lax.all_to_all(
        sent, ("section", "seq"), 0, 0, axis_index_groups=SHARED_XY
    )
    back = pl.pallas_call(
        combine_kernel,
        out_shape=jax.ShapeDtypeStruct((LAYERS, 64, HQ * HD), jnp.bfloat16),
        in_specs=[sspec(), vspec(), vspec(), vspec()],
        out_specs=vspec(),
        name="combine",
    )(section[None], got, residual_in, gains)
    mine = lax.all_to_all(back, "section", 0, 0)
    return mine.reshape(1, ROWS, HQ * HD)


def solution(mesh):
    placed = (
        P("section", "seq", None),
        P("section", "seq", None),
        P("section", "seq", None),
        P("seq"),
        P("seq"),
        P("seq", None),
        P("section", None),
    )
    return jax.shard_map(
        per_device, mesh=mesh, in_specs=placed, out_specs=P("section", "seq", None), check_vma=False
    )
```

```python
import functools
import math

import jax
import jax.numpy as jnp
from jax import lax
from jax.experimental import pallas as pl
from jax.experimental.pallas import tpu as pltpu
from jax.sharding import PartitionSpec as P

HQ = 8
HK = 4
HD = 256
WINDOW = 4096
ROWS = 256
PLANE = 2048
LAYERS = 4
HALF = HD // 2
VMEM = pltpu.VMEM
CAP = 50.0 / math.log(2.0)

SHARED_Y = [[z * 8 + y * 2 + c for y in range(4)] for z in range(8) for c in range(2)]
SHARED_XY = [
    [x * 64 + z * 8 + y * 2 + c for x in range(4) for y in range(4)]
    for z in range(8)
    for c in range(2)
]
NEXT_PLANE = [(i, i + 8) for i in range(56)]
OTHER_CORE = [(i, i ^ 1) for i in range(64)]


def vspec():
    return pl.BlockSpec(memory_space=VMEM)


def turned(x, cosine, sine):
    first = x[:, :HALF].astype(jnp.float32)
    second = x[:, HALF:].astype(jnp.float32)
    return (
        (first * cosine - second * sine).astype(jnp.bfloat16),
        (second * cosine + first * sine).astype(jnp.bfloat16),
    )


def rotate_kv_kernel(cos_ref, sin_ref, k_ref, v_ref, km_ref, vm_ref):
    for h in range(HK):
        a, b = turned(k_ref[:, h * HD : (h + 1) * HD], cos_ref[...], sin_ref[...])
        km_ref[h, :, :HALF] = a
        km_ref[h, :, HALF:] = b
        vm_ref[h] = v_ref[:, h * HD : (h + 1) * HD]


def rotate_q_kernel(cos_ref, sin_ref, place_ref, q_ref, qm_ref):
    for h in range(HQ):
        a, b = turned(q_ref[:, h * HD : (h + 1) * HD], cos_ref[...], sin_ref[...])
        rows = pl.ds((h % 2) * ROWS, ROWS)
        qm_ref[h // 2, rows, :HALF] = a
        qm_ref[h // 2, rows, HALF:] = b
    for h in range(HK):
        qm_ref[h, 2 * ROWS :] = place_ref[...]


def attend_kernel(back, q_ref, k_own, k_oth, v_own, v_oth, *refs):
    if back == 0:
        num, den = refs
    elif back == 1:
        num_in, den_in, num, den = refs
    else:
        num_in, den_in, out_ref = refs
    block = pl.program_id(0)
    device = lax.axis_index("seq")
    plane0 = device // 8 * PLANE
    core = lax.rem(device, 2)
    keys0 = plane0 - back * PLANE

    def sums(r):
        begin, end = {0: (0, r + 1), 1: (0, 4), 2: (r, 4)}[back]
        count = (end - begin) * ROWS
        query = q_ref[0, : 2 * ROWS]
        split = q_ref[0, 2 * ROWS :].astype(jnp.float32)
        place = (split[0:1] * 128.0 + split[1:2]).astype(jnp.int32)
        token = plane0 + r * 512 + core * ROWS + lax.broadcasted_iota(jnp.int32, (1, ROWS), 1)
        low = token - jnp.minimum(place, WINDOW - 1)
        low = jnp.transpose(jnp.broadcast_to(low, (HALF, ROWS)))
        low = jnp.concatenate([low, low], axis=0)
        low = jnp.concatenate([low] * (count // HALF), axis=1)
        col = lax.broadcasted_iota(jnp.int32, (1, count), 1)
        spread = col + lax.shift_right_logical(col, 8) * ROWS + begin * 512 + keys0
        total, added = None, None
        for k_ref, v_ref, side in ((k_own, v_own, core), (k_oth, v_oth, 1 - core)):
            score = lax.dot_general(
                query,
                k_ref[begin:end].reshape(count, HD),
                (((1,), (1,)), ((), ())),
                preferred_element_type=jnp.float32,
            )
            weight = jnp.exp2(jnp.tanh(score * (1.0 / 800.0)) * CAP)
            key = spread + side * ROWS
            ok = key >= low
            if back == 0:
                row = lax.broadcasted_iota(jnp.int32, (2 * ROWS, 1), 0) & (ROWS - 1)
                ok = ok & (key <= plane0 + r * 512 + core * ROWS + row)
            weight = jnp.where(ok, weight, 0.0)
            lanes = sum(weight[:, i * HALF : (i + 1) * HALF] for i in range(count // HALF))
            part = jnp.dot(
                weight.astype(jnp.bfloat16),
                v_ref[begin:end].reshape(count, HD),
                preferred_element_type=jnp.float32,
            )
            total = lanes if total is None else total + lanes
            added = part if added is None else added + part
        return total, added

    def finish(total, added):
        if back == 0:
            num[0] = added
            den[0] = total
        elif back == 1:
            num[0] = num_in[0] + added
            den[0] = den_in[0] + total
        else:
            whole = (num_in[0] + added) / jnp.sum(den_in[0] + total, axis=-1, keepdims=True)
            whole = whole.astype(jnp.bfloat16)
            for q in range(4):
                for h in range(2):
                    first = h * ROWS + q * 64
                    out_ref[q, 0, :, h * HD : (h + 1) * HD] = whole[first : first + 64]

    for r in range(4):

        @pl.when(block == r)
        def _():
            finish(*sums(r))


def attend(back, query, k_own, k_oth, v_own, v_oth, num, den):
    def step(*shape):
        return pl.BlockSpec((1,) + shape, lambda i: (i,) + (0,) * len(shape))

    whole = pl.BlockSpec(
        (4, ROWS, HD), lambda i: (0, 0, 0), pipeline_mode=pl.Buffered(1)
    )
    args = [query, k_own, k_oth, v_own, v_oth]
    in_specs = [step(2 * ROWS + 16, HD)] + [whole] * 4
    aliases = {}
    outs = [
        jax.ShapeDtypeStruct((4, 512, HD), jnp.float32),
        jax.ShapeDtypeStruct((4, 512, HALF), jnp.float32),
    ]
    out_specs = [step(512, HD), step(512, HALF)]
    if back:
        args += [num, den]
        in_specs += [step(512, HD), step(512, HALF)]
    if back == 1:
        aliases = {5: 0, 6: 1}
    if back == 2:
        outs = jax.ShapeDtypeStruct((4, 4, 64, 512), jnp.bfloat16)
        out_specs = pl.BlockSpec((4, 1, 64, 512), lambda i: (0, i, 0, 0))
    pairs = {0: 20, 1: 32, 2: 20}[back]
    return pl.pallas_call(
        functools.partial(attend_kernel, back),
        grid=(4,),
        out_shape=outs,
        in_specs=in_specs,
        out_specs=out_specs,
        input_output_aliases=aliases,
        compiler_params=pltpu.CompilerParams(
            vmem_limit_bytes=48 << 20, dimension_semantics=("arbitrary",)
        ),
        cost_estimate=pl.CostEstimate(
            flops=pairs * 512 * 256 * 256 * 4 * 3,
            bytes_accessed=8 << 20,
            transcendentals=pairs * 512 * 256 * 2,
        ),
        name="attend_%d" % back,
    )(*args)


def combine_kernel(got_ref, res_ref, g0_ref, g1_ref, g2_ref, g3_ref, out_ref, gain_ref):
    section = lax.axis_index("section")
    for r, ref in enumerate((g0_ref, g1_ref, g2_ref, g3_ref)):
        gain_ref[pl.ds(lax.rem(section + 4 - r, 4), 1), :] = ref[...]
    rows = pl.ds(pl.multiple_of(section * 64, 64), 64)
    running = res_ref[rows, :].astype(jnp.float32)
    running = [running[:, h * 512 : (h + 1) * 512] for h in range(4)]
    for layer in range(LAYERS):
        parts = [got_ref[layer * 4 + h].astype(jnp.float32) for h in range(4)]
        square = sum(jnp.sum(p * p, axis=-1, keepdims=True) for p in parts)
        norm = lax.rsqrt(square * (1.0 / (HQ * HD)) + 1e-06)
        for h in range(4):
            gain = gain_ref[layer : layer + 1, h * 512 : (h + 1) * 512]
            running[h] = running[h] + parts[h] * norm * gain
            out_ref[layer, :, h * 512 : (h + 1) * 512] = running[h].astype(jnp.bfloat16)


def per_device(queries, keys, values, segment_ids, positions, residual_in, post_gain):
    inverse = jnp.exp(-math.log(10000.0) * jnp.arange(HALF).astype(jnp.float32) / HALF)
    angle = positions.astype(jnp.float32)[:, None] * inverse[None, :]
    cosine = jnp.cos(angle)
    sine = jnp.sin(angle)
    split = jnp.stack([lax.shift_right_logical(positions, 7), positions & 127])
    places = jnp.concatenate([split, jnp.zeros((14, ROWS), jnp.int32)]).astype(jnp.bfloat16)

    def over_y(x):
        return lax.all_to_all(x, "seq", 0, 0, axis_index_groups=SHARED_Y)

    def onward(x):
        return lax.ppermute(x, "seq", NEXT_PLANE)

    def other(x):
        return lax.ppermute(x, "seq", OTHER_CORE)

    gains = [post_gain] + [
        lax.ppermute(post_gain, "section", [(i, (i + r) % 4) for i in range(4)])
        for r in (1, 2, 3)
    ]
    k_msg, v_msg = pl.pallas_call(
        rotate_kv_kernel,
        out_shape=[jax.ShapeDtypeStruct((HK, ROWS, HD), jnp.bfloat16)] * 2,
        in_specs=[vspec()] * 4,
        out_specs=[vspec()] * 2,
        name="rotate_kv",
    )(cosine, sine, keys[0], values[0])
    q_msg = pl.pallas_call(
        rotate_q_kernel,
        out_shape=jax.ShapeDtypeStruct((HK, 2 * ROWS + 16, HD), jnp.bfloat16),
        in_specs=[vspec()] * 4,
        out_specs=vspec(),
        name="rotate_q",
    )(cosine, sine, places, queries[0])

    k0 = over_y(k_msg)
    v0 = over_y(v_msg)
    query = over_y(q_msg)
    k1 = onward(k0)
    v1 = onward(v0)
    k2 = onward(k1)
    v2 = onward(v1)

    num, den = attend(0, query, k0, other(k0), v0, other(v0), None, None)
    num, den = attend(1, query, k1, other(k1), v1, other(v1), num, den)
    num, den, k2, v2 = lax.optimization_barrier((num, den, k2, v2))
    sent = attend(2, query, k2, other(k2), v2, other(v2), num, den)
    got = lax.all_to_all(
        sent.reshape(16, 64, 512), ("section", "seq"), 0, 0, axis_index_groups=SHARED_XY
    )
    back = pl.pallas_call(
        combine_kernel,
        out_shape=jax.ShapeDtypeStruct((LAYERS, 64, HQ * HD), jnp.bfloat16),
        in_specs=[vspec()] * 6,
        out_specs=vspec(),
        scratch_shapes=[VMEM((LAYERS, HQ * HD), jnp.float32)],
        name="combine",
    )(got, residual_in, *gains)
    mine = lax.all_to_all(back, "section", 0, 0)
    return mine.reshape(1, ROWS, HQ * HD)


def solution(mesh):
    placed = (
        P("section", "seq", None),
        P("section", "seq", None),
        P("section", "seq", None),
        P("seq"),
        P("seq"),
        P("seq", None),
        P("section", None),
    )
    return jax.shard_map(
        per_device, mesh=mesh, in_specs=placed, out_specs=P("section", "seq", None), check_vma=False
    )
```

```python
import functools
import math

import jax
import jax.numpy as jnp
from jax import lax
from jax.experimental import pallas as pl
from jax.experimental.pallas import tpu as pltpu
from jax.sharding import PartitionSpec as P

HQ = 8
HK = 4
HD = 256
WINDOW = 4096
ROWS = 256
PLANE = 2048
LAYERS = 4
HALF = HD // 2
VMEM = pltpu.VMEM
CAP = 50.0 / math.log(2.0)

SHARED_Y = [[z * 8 + y * 2 + c for y in range(4)] for z in range(8) for c in range(2)]
SHARED_XY = [
    [x * 64 + z * 8 + y * 2 + c for x in range(4) for y in range(4)]
    for z in range(8)
    for c in range(2)
]
NEXT_PLANE = [(i, i + 8) for i in range(56)]
OTHER_CORE = [(i, i ^ 1) for i in range(64)]


def vspec():
    return pl.BlockSpec(memory_space=VMEM)


def turned(x, cosine, sine):
    first = x[:, :HALF].astype(jnp.float32)
    second = x[:, HALF:].astype(jnp.float32)
    return (
        (first * cosine - second * sine).astype(jnp.bfloat16),
        (second * cosine + first * sine).astype(jnp.bfloat16),
    )


def split_v_kernel(v_ref, vm_ref):
    for h in range(HK):
        vm_ref[h] = v_ref[:, h * HD : (h + 1) * HD]


def rotate_k_kernel(cos_ref, sin_ref, k_ref, km_ref):
    for h in range(HK):
        a, b = turned(k_ref[:, h * HD : (h + 1) * HD], cos_ref[...], sin_ref[...])
        km_ref[h, :, :HALF] = a
        km_ref[h, :, HALF:] = b


def rotate_q_kernel(cos_ref, sin_ref, place_ref, q_ref, qm_ref):
    for h in range(HQ):
        a, b = turned(q_ref[:, h * HD : (h + 1) * HD], cos_ref[...], sin_ref[...])
        rows = pl.ds((h % 2) * ROWS, ROWS)
        qm_ref[h // 2, rows, :HALF] = a
        qm_ref[h // 2, rows, HALF:] = b
    for h in range(HK):
        qm_ref[h, 2 * ROWS :] = place_ref[...]


def attend_kernel(back, q_ref, k_own, k_oth, v_own, v_oth, *refs):
    if back == 0:
        num, den = refs
    elif back == 1:
        num_in, den_in, num, den = refs
    else:
        num_in, den_in, out_ref = refs
    device = lax.axis_index("seq")
    plane0 = device // 8 * PLANE
    core = lax.rem(device, 2)
    keys0 = plane0 - back * PLANE
    for r in range(4):
        begin, end = {0: (0, r + 1), 1: (0, 4), 2: (r, 4)}[back]
        count = (end - begin) * ROWS
        query = q_ref[r, : 2 * ROWS]
        split = q_ref[r, 2 * ROWS :].astype(jnp.float32)
        place = (split[0:1] * 128.0 + split[1:2]).astype(jnp.int32)
        token = plane0 + r * 512 + core * ROWS + lax.broadcasted_iota(jnp.int32, (1, ROWS), 1)
        low = token - jnp.minimum(place, WINDOW - 1)
        low = jnp.transpose(jnp.broadcast_to(low, (HALF, ROWS)))
        low = jnp.concatenate([low, low], axis=0)
        low = jnp.concatenate([low] * (count // HALF), axis=1)
        col = lax.broadcasted_iota(jnp.int32, (1, count), 1)
        spread = col + lax.shift_right_logical(col, 8) * ROWS + begin * 512 + keys0
        total, added = None, None
        for k_ref, v_ref, side in ((k_own, v_own, core), (k_oth, v_oth, 1 - core)):
            score = lax.dot_general(
                query,
                k_ref[begin:end].reshape(count, HD),
                (((1,), (1,)), ((), ())),
                preferred_element_type=jnp.float32,
            )
            weight = jnp.exp2(jnp.tanh(score * (1.0 / 800.0)) * CAP)
            key = spread + side * ROWS
            ok = key >= low
            if back == 0:
                row = lax.broadcasted_iota(jnp.int32, (2 * ROWS, 1), 0) & (ROWS - 1)
                ok = ok & (key <= plane0 + r * 512 + core * ROWS + row)
            weight = jnp.where(ok, weight, 0.0)
            lanes = sum(weight[:, i * HALF : (i + 1) * HALF] for i in range(count // HALF))
            part = jnp.dot(
                weight.astype(jnp.bfloat16),
                v_ref[begin:end].reshape(count, HD),
                preferred_element_type=jnp.float32,
            )
            total = lanes if total is None else total + lanes
            added = part if added is None else added + part
        if back == 0:
            num[r] = added
            den[r] = total
        elif back == 1:
            num[r] = num_in[r] + added
            den[r] = den_in[r] + total
        else:
            scale = 1.0 / jnp.sum(den_in[r] + total, axis=-1, keepdims=True)
            whole = ((num_in[r] + added) * scale).astype(jnp.bfloat16)
            for q in range(4):
                for h in range(2):
                    first = h * ROWS + q * 64
                    out_ref[q, r, :, h * HD : (h + 1) * HD] = whole[first : first + 64]


def attend(back, query, k_own, k_oth, v_own, v_oth, num, den):
    args = [query, k_own, k_oth, v_own, v_oth]
    aliases = {}
    outs = [
        jax.ShapeDtypeStruct((4, 512, HD), jnp.float32),
        jax.ShapeDtypeStruct((4, 512, HALF), jnp.float32),
    ]
    out_specs = [vspec(), vspec()]
    if back:
        args += [num, den]
    if back == 1:
        aliases = {5: 0, 6: 1}
    if back == 2:
        outs = jax.ShapeDtypeStruct((4, 4, 64, 512), jnp.bfloat16)
        out_specs = vspec()
    pairs = {0: 20, 1: 32, 2: 20}[back]
    return pl.pallas_call(
        functools.partial(attend_kernel, back),
        out_shape=outs,
        in_specs=[vspec()] * len(args),
        out_specs=out_specs,
        input_output_aliases=aliases,
        compiler_params=pltpu.CompilerParams(vmem_limit_bytes=40 << 20),
        cost_estimate=pl.CostEstimate(
            flops=pairs * 512 * 256 * 256 * 4 * 2,
            bytes_accessed=8 << 20,
            transcendentals=pairs * 512 * 256 * 2,
        ),
        name="attend_%d" % back,
    )(*args)


def combine_kernel(got_ref, res_ref, g0_ref, g1_ref, g2_ref, g3_ref, out_ref, gain_ref):
    section = lax.axis_index("section")
    for r, ref in enumerate((g0_ref, g1_ref, g2_ref, g3_ref)):
        gain_ref[pl.ds(lax.rem(section + 4 - r, 4), 1), :] = ref[...]
    rows = pl.ds(pl.multiple_of(section * 64, 64), 64)
    running = res_ref[rows, :].astype(jnp.float32)
    running = [running[:, h * 512 : (h + 1) * 512] for h in range(4)]
    for layer in range(LAYERS):
        parts = [got_ref[layer * 4 + h].astype(jnp.float32) for h in range(4)]
        square = sum(jnp.sum(p * p, axis=-1, keepdims=True) for p in parts)
        norm = lax.rsqrt(square * (1.0 / (HQ * HD)) + 1e-06)
        for h in range(4):
            gain = gain_ref[layer : layer + 1, h * 512 : (h + 1) * 512]
            running[h] = running[h] + parts[h] * norm * gain
            out_ref[layer, :, h * 512 : (h + 1) * 512] = running[h].astype(jnp.bfloat16)


def per_device(queries, keys, values, segment_ids, positions, residual_in, post_gain):
    inverse = jnp.exp(-math.log(10000.0) * jnp.arange(HALF).astype(jnp.float32) / HALF)
    angle = positions.astype(jnp.float32)[:, None] * inverse[None, :]
    cosine = jnp.cos(angle)
    sine = jnp.sin(angle)
    split = jnp.stack([lax.shift_right_logical(positions, 7), positions & 127])
    places = jnp.concatenate([split, jnp.zeros((14, ROWS), jnp.int32)]).astype(jnp.bfloat16)

    def over_y(x):
        return lax.all_to_all(x, "seq", 0, 0, axis_index_groups=SHARED_Y)

    def onward(x):
        return lax.ppermute(x, "seq", NEXT_PLANE)

    def other(x):
        return lax.ppermute(x, "seq", OTHER_CORE)

    gains = [post_gain] + [
        lax.ppermute(post_gain, "section", [(i, (i + r) % 4) for i in range(4)])
        for r in (1, 2, 3)
    ]
    v_msg = pl.pallas_call(
        split_v_kernel,
        out_shape=jax.ShapeDtypeStruct((HK, ROWS, HD), jnp.bfloat16),
        in_specs=[vspec()],
        out_specs=vspec(),
        name="split_v",
    )(values[0])
    k_msg = pl.pallas_call(
        rotate_k_kernel,
        out_shape=jax.ShapeDtypeStruct((HK, ROWS, HD), jnp.bfloat16),
        in_specs=[vspec()] * 3,
        out_specs=vspec(),
        name="rotate_k",
    )(cosine, sine, keys[0])
    q_msg = pl.pallas_call(
        rotate_q_kernel,
        out_shape=jax.ShapeDtypeStruct((HK, 2 * ROWS + 16, HD), jnp.bfloat16),
        in_specs=[vspec()] * 4,
        out_specs=vspec(),
        name="rotate_q",
    )(cosine, sine, places, queries[0])

    v0 = over_y(v_msg)
    v0, k_msg = lax.optimization_barrier((v0, k_msg))
    v1 = onward(v0)
    k0 = over_y(k_msg)
    k1 = onward(k0)
    v1, q_msg = lax.optimization_barrier((v1, q_msg))
    query = over_y(q_msg)
    v2 = onward(v1)
    k2 = onward(k1)

    num, den = attend(0, query, k0, other(k0), v0, other(v0), None, None)
    num, den = attend(1, query, k1, other(k1), v1, other(v1), num, den)
    num, den, k2, v2 = lax.optimization_barrier((num, den, k2, v2))
    sent = attend(2, query, k2, other(k2), v2, other(v2), num, den)
    got = lax.all_to_all(
        sent.reshape(16, 64, 512), ("section", "seq"), 0, 0, axis_index_groups=SHARED_XY
    )
    back = pl.pallas_call(
        combine_kernel,
        out_shape=jax.ShapeDtypeStruct((LAYERS, 64, HQ * HD), jnp.bfloat16),
        in_specs=[vspec()] * 6,
        out_specs=vspec(),
        scratch_shapes=[VMEM((LAYERS, HQ * HD), jnp.float32)],
        name="combine",
    )(got, residual_in, *gains)
    mine = lax.all_to_all(back, "section", 0, 0)
    return mine.reshape(1, ROWS, HQ * HD)


def solution(mesh):
    placed = (
        P("section", "seq", None),
        P("section", "seq", None),
        P("section", "seq", None),
        P("seq"),
        P("seq"),
        P("seq", None),
        P("section", None),
    )
    return jax.shard_map(
        per_device, mesh=mesh, in_specs=placed, out_specs=P("section", "seq", None), check_vma=False
    )
```

```python
import functools
import math

import jax
import jax.numpy as jnp
from jax import lax
from jax.experimental import pallas as pl
from jax.experimental.pallas import tpu as pltpu
from jax.sharding import PartitionSpec as P

HQ = 8
HK = 4
HD = 256
WINDOW = 4096
ROWS = 256
PLANE = 2048
LAYERS = 4
HALF = HD // 2
VMEM = pltpu.VMEM
CAP = 50.0 / math.log(2.0)

SHARED_Y = [[z * 8 + y * 2 + c for y in range(4)] for z in range(8) for c in range(2)]
SHARED_XY = [
    [x * 64 + z * 8 + y * 2 + c for x in range(4) for y in range(4)]
    for z in range(8)
    for c in range(2)
]
NEXT_PLANE = [(i, i + 8) for i in range(56)]
OTHER_CORE = [(i, i ^ 1) for i in range(64)]


def vspec():
    return pl.BlockSpec(memory_space=VMEM)


def turned(x, cosine, sine):
    first = x[:, :HALF].astype(jnp.float32)
    second = x[:, HALF:].astype(jnp.float32)
    return (
        (first * cosine - second * sine).astype(jnp.bfloat16),
        (second * cosine + first * sine).astype(jnp.bfloat16),
    )


def split_v_kernel(v_ref, vm_ref):
    for h in range(HK):
        vm_ref[h] = v_ref[:, h * HD : (h + 1) * HD]


def rotate_k_kernel(cos_ref, sin_ref, k_ref, km_ref):
    for h in range(HK):
        a, b = turned(k_ref[:, h * HD : (h + 1) * HD], cos_ref[...], sin_ref[...])
        km_ref[h, :, :HALF] = a
        km_ref[h, :, HALF:] = b


def rotate_q_kernel(cos_ref, sin_ref, place_ref, q_ref, qm_ref):
    for h in range(HQ):
        a, b = turned(q_ref[:, h * HD : (h + 1) * HD], cos_ref[...], sin_ref[...])
        rows = pl.ds((h % 2) * ROWS, ROWS)
        qm_ref[h // 2, rows, :HALF] = a
        qm_ref[h // 2, rows, HALF:] = b
    for h in range(HK):
        qm_ref[h, 2 * ROWS :] = place_ref[...]


def attend_kernel(back, q_ref, k_own, k_oth, v_own, v_oth, *refs):
    if back == 0:
        num, den = refs
    elif back == 1:
        num_in, den_in, num, den = refs
    else:
        num_in, den_in, out_ref = refs
    device = lax.axis_index("seq")
    plane0 = device // 8 * PLANE
    core = lax.rem(device, 2)
    keys0 = plane0 - back * PLANE
    for r in range(4):
        begin, end = {0: (0, r + 1), 1: (0, 4), 2: (r, 4)}[back]
        count = (end - begin) * ROWS
        query = q_ref[r, : 2 * ROWS]
        split = q_ref[r, 2 * ROWS :].astype(jnp.float32)
        place = (split[0:1] * 128.0 + split[1:2]).astype(jnp.int32)
        token = plane0 + r * 512 + core * ROWS + lax.broadcasted_iota(jnp.int32, (1, ROWS), 1)
        low = token - jnp.minimum(place, WINDOW - 1)
        low = jnp.transpose(jnp.broadcast_to(low, (HALF, ROWS)))
        low = jnp.concatenate([low, low], axis=0)
        low = jnp.concatenate([low] * (count // HALF), axis=1)
        col = lax.broadcasted_iota(jnp.int32, (1, count), 1)
        spread = col + lax.shift_right_logical(col, 8) * ROWS + begin * 512 + keys0
        total, added = None, None
        for k_ref, v_ref, side in ((k_own, v_own, core), (k_oth, v_oth, 1 - core)):
            score = lax.dot_general(
                query,
                k_ref[begin:end].reshape(count, HD),
                (((1,), (1,)), ((), ())),
                preferred_element_type=jnp.float32,
            )
            weight = jnp.exp2(jnp.tanh(score * (1.0 / 800.0)) * CAP)
            key = spread + side * ROWS
            ok = key >= low
            if back == 0:
                row = lax.broadcasted_iota(jnp.int32, (2 * ROWS, 1), 0) & (ROWS - 1)
                ok = ok & (key <= plane0 + r * 512 + core * ROWS + row)
            weight = jnp.where(ok, weight, 0.0)
            lanes = sum(weight[:, i * HALF : (i + 1) * HALF] for i in range(count // HALF))
            part = jnp.dot(
                weight.astype(jnp.bfloat16),
                v_ref[begin:end].reshape(count, HD),
                preferred_element_type=jnp.float32,
            )
            total = lanes if total is None else total + lanes
            added = part if added is None else added + part
        if back == 0:
            num[r] = added
            den[r] = total
        elif back == 1:
            num[r] = num_in[r] + added
            den[r] = den_in[r] + total
        else:
            scale = 1.0 / jnp.sum(den_in[r] + total, axis=-1, keepdims=True)
            whole = ((num_in[r] + added) * scale).astype(jnp.bfloat16)
            for q in range(4):
                for h in range(2):
                    first = h * ROWS + q * 64
                    out_ref[q, r, :, h * HD : (h + 1) * HD] = whole[first : first + 64]


def attend(back, query, k_own, k_oth, v_own, v_oth, num, den):
    args = [query, k_own, k_oth, v_own, v_oth]
    aliases = {}
    outs = [
        jax.ShapeDtypeStruct((4, 512, HD), jnp.float32),
        jax.ShapeDtypeStruct((4, 512, HALF), jnp.float32),
    ]
    out_specs = [vspec(), vspec()]
    if back:
        args += [num, den]
    if back == 1:
        aliases = {5: 0, 6: 1}
    if back == 2:
        outs = jax.ShapeDtypeStruct((4, 4, 64, 512), jnp.bfloat16)
        out_specs = vspec()
    pairs = {0: 20, 1: 32, 2: 20}[back]
    return pl.pallas_call(
        functools.partial(attend_kernel, back),
        out_shape=outs,
        in_specs=[vspec()] * len(args),
        out_specs=out_specs,
        input_output_aliases=aliases,
        compiler_params=pltpu.CompilerParams(vmem_limit_bytes=24 << 20),
        cost_estimate=pl.CostEstimate(
            flops=pairs * 512 * 256 * 256 * 4 * 2,
            bytes_accessed=8 << 20,
            transcendentals=pairs * 512 * 256 * 2,
        ),
        name="attend_%d" % back,
    )(*args)


def combine_kernel(got_ref, res_ref, g0_ref, g1_ref, g2_ref, g3_ref, out_ref, gain_ref):
    section = lax.axis_index("section")
    for r, ref in enumerate((g0_ref, g1_ref, g2_ref, g3_ref)):
        gain_ref[pl.ds(lax.rem(section + 4 - r, 4), 1), :] = ref[...]
    rows = pl.ds(pl.multiple_of(section * 64, 64), 64)
    running = res_ref[rows, :].astype(jnp.float32)
    running = [running[:, h * 512 : (h + 1) * 512] for h in range(4)]
    for layer in range(LAYERS):
        parts = [got_ref[layer * 4 + h].astype(jnp.float32) for h in range(4)]
        square = sum(jnp.sum(p * p, axis=-1, keepdims=True) for p in parts)
        norm = lax.rsqrt(square * (1.0 / (HQ * HD)) + 1e-06)
        for h in range(4):
            gain = gain_ref[layer : layer + 1, h * 512 : (h + 1) * 512]
            running[h] = running[h] + parts[h] * norm * gain
            out_ref[layer, :, h * 512 : (h + 1) * 512] = running[h].astype(jnp.bfloat16)


def per_device(queries, keys, values, segment_ids, positions, residual_in, post_gain):
    inverse = jnp.exp(-math.log(10000.0) * jnp.arange(HALF).astype(jnp.float32) / HALF)
    angle = positions.astype(jnp.float32)[:, None] * inverse[None, :]
    cosine = jnp.cos(angle)
    sine = jnp.sin(angle)
    split = jnp.stack([lax.shift_right_logical(positions, 7), positions & 127])
    places = jnp.concatenate([split, jnp.zeros((14, ROWS), jnp.int32)]).astype(jnp.bfloat16)

    def over_y(x):
        return lax.all_to_all(x, "seq", 0, 0, axis_index_groups=SHARED_Y)

    def onward(x):
        return lax.ppermute(x, "seq", NEXT_PLANE)

    def other(x):
        return lax.ppermute(x, "seq", OTHER_CORE)

    gains = [post_gain] + [
        lax.ppermute(post_gain, "section", [(i, (i + r) % 4) for i in range(4)])
        for r in (1, 2, 3)
    ]
    v_msg = pl.pallas_call(
        split_v_kernel,
        out_shape=jax.ShapeDtypeStruct((HK, ROWS, HD), jnp.bfloat16),
        in_specs=[vspec()],
        out_specs=vspec(),
        name="split_v",
    )(values[0])
    k_msg = pl.pallas_call(
        rotate_k_kernel,
        out_shape=jax.ShapeDtypeStruct((HK, ROWS, HD), jnp.bfloat16),
        in_specs=[vspec()] * 3,
        out_specs=vspec(),
        name="rotate_k",
    )(cosine, sine, keys[0])
    q_msg = pl.pallas_call(
        rotate_q_kernel,
        out_shape=jax.ShapeDtypeStruct((HK, 2 * ROWS + 16, HD), jnp.bfloat16),
        in_specs=[vspec()] * 4,
        out_specs=vspec(),
        name="rotate_q",
    )(cosine, sine, places, queries[0])

    v0 = over_y(v_msg)
    v0, k_msg = lax.optimization_barrier((v0, k_msg))
    v1 = onward(v0)
    k0 = over_y(k_msg)
    k1 = onward(k0)
    v1, q_msg = lax.optimization_barrier((v1, q_msg))
    query = over_y(q_msg)
    v2 = onward(v1)
    query, v2 = lax.optimization_barrier((query, v2))
    k2 = onward(k1)

    num, den = attend(0, query, k0, other(k0), v0, other(v0), None, None)
    num, den = attend(1, query, k1, other(k1), v1, other(v1), num, den)
    num, den, k2 = lax.optimization_barrier((num, den, k2))
    sent = attend(2, query, k2, other(k2), v2, other(v2), num, den)
    got = lax.all_to_all(
        sent.reshape(16, 64, 512), ("section", "seq"), 0, 0, axis_index_groups=SHARED_XY
    )
    back = pl.pallas_call(
        combine_kernel,
        out_shape=jax.ShapeDtypeStruct((LAYERS, 64, HQ * HD), jnp.bfloat16),
        in_specs=[vspec()] * 6,
        out_specs=vspec(),
        scratch_shapes=[VMEM((LAYERS, HQ * HD), jnp.float32)],
        name="combine",
    )(got, residual_in, *gains)
    mine = lax.all_to_all(back, "section", 0, 0)
    return mine.reshape(1, ROWS, HQ * HD)


def solution(mesh):
    placed = (
        P("section", "seq", None),
        P("section", "seq", None),
        P("section", "seq", None),
        P("seq"),
        P("seq"),
        P("seq", None),
        P("section", None),
    )
    return jax.shard_map(
        per_device, mesh=mesh, in_specs=placed, out_specs=P("section", "seq", None), check_vma=False
    )
```

```python
import functools
import math

import jax
import jax.numpy as jnp
from jax import lax
from jax.experimental import pallas as pl
from jax.experimental.pallas import tpu as pltpu
from jax.sharding import PartitionSpec as P

HQ = 8
HK = 4
HD = 256
WINDOW = 4096
ROWS = 256
PLANE = 2048
LAYERS = 4
HALF = HD // 2
VMEM = pltpu.VMEM
CAP = 50.0 / math.log(2.0)

SHARED_Y = [[z * 8 + y * 2 + c for y in range(4)] for z in range(8) for c in range(2)]
SHARED_XY = [
    [x * 64 + z * 8 + y * 2 + c for x in range(4) for y in range(4)]
    for z in range(8)
    for c in range(2)
]
NEXT_PLANE = [(i, i + 8) for i in range(56)]
OTHER_CORE = [(i, i ^ 1) for i in range(64)]


def vspec():
    return pl.BlockSpec(memory_space=VMEM)


def turned(x, cosine, sine):
    first = x[:, :HALF].astype(jnp.float32)
    second = x[:, HALF:].astype(jnp.float32)
    return (
        (first * cosine - second * sine).astype(jnp.bfloat16),
        (second * cosine + first * sine).astype(jnp.bfloat16),
    )


def split_v_kernel(v_ref, vm_ref):
    for h in range(HK):
        vm_ref[h] = v_ref[:, h * HD : (h + 1) * HD]


def rotate_k_kernel(cos_ref, sin_ref, k_ref, km_ref):
    for h in range(HK):
        a, b = turned(k_ref[:, h * HD : (h + 1) * HD], cos_ref[...], sin_ref[...])
        km_ref[h, :, :HALF] = a
        km_ref[h, :, HALF:] = b


def rotate_q_kernel(cos_ref, sin_ref, place_ref, q_ref, qm_ref):
    for h in range(HQ):
        a, b = turned(q_ref[:, h * HD : (h + 1) * HD], cos_ref[...], sin_ref[...])
        rows = pl.ds((h % 2) * ROWS, ROWS)
        qm_ref[h // 2, rows, :HALF] = a
        qm_ref[h // 2, rows, HALF:] = b
    for h in range(HK):
        qm_ref[h, 2 * ROWS :] = place_ref[...]


def attend_kernel(back, q_ref, k_own, k_oth, v_own, v_oth, *refs):
    if back == 0:
        num, den = refs
    elif back == 1:
        num_in, den_in, num, den = refs
    else:
        num_in, den_in, out_ref = refs
    device = lax.axis_index("seq")
    plane0 = device // 8 * PLANE
    core = lax.rem(device, 2)
    keys0 = plane0 - back * PLANE
    for r in range(4):
        begin, end = {0: (0, r + 1), 1: (0, 4), 2: (r, 4)}[back]
        count = (end - begin) * ROWS
        query = q_ref[r, : 2 * ROWS]
        split = q_ref[r, 2 * ROWS :].astype(jnp.float32)
        place = (split[0:1] * 128.0 + split[1:2]).astype(jnp.int32)
        token = plane0 + r * 512 + core * ROWS + lax.broadcasted_iota(jnp.int32, (1, ROWS), 1)
        low = token - jnp.minimum(place, WINDOW - 1)
        low = jnp.transpose(jnp.broadcast_to(low, (HALF, ROWS)))
        low = jnp.concatenate([low, low], axis=0)
        low = jnp.concatenate([low] * (count // HALF), axis=1)
        col = lax.broadcasted_iota(jnp.int32, (1, count), 1)
        spread = col + lax.shift_right_logical(col, 8) * ROWS + begin * 512 + keys0
        total, added = None, None
        for k_ref, v_ref, side in ((k_own, v_own, core), (k_oth, v_oth, 1 - core)):
            score = lax.dot_general(
                query,
                k_ref[begin:end].reshape(count, HD),
                (((1,), (1,)), ((), ())),
                preferred_element_type=jnp.float32,
            )
            weight = jnp.exp2(jnp.tanh(score * (1.0 / 800.0)) * CAP)
            key = spread + side * ROWS
            ok = key >= low
            if back == 0:
                row = lax.broadcasted_iota(jnp.int32, (2 * ROWS, 1), 0) & (ROWS - 1)
                ok = ok & (key <= plane0 + r * 512 + core * ROWS + row)
            weight = jnp.where(ok, weight, 0.0)
            lanes = sum(weight[:, i * HALF : (i + 1) * HALF] for i in range(count // HALF))
            part = jnp.dot(
                weight.astype(jnp.bfloat16),
                v_ref[begin:end].reshape(count, HD),
                preferred_element_type=jnp.float32,
            )
            total = lanes if total is None else total + lanes
            added = part if added is None else added + part
        if back == 0:
            num[r] = added
            den[r] = total
        elif back == 1:
            num[r] = num_in[r] + added
            den[r] = den_in[r] + total
        else:
            scale = 1.0 / jnp.sum(den_in[r] + total, axis=-1, keepdims=True)
            whole = ((num_in[r] + added) * scale).astype(jnp.bfloat16)
            for q in range(4):
                for h in range(2):
                    first = h * ROWS + q * 64
                    out_ref[q, r, :, h * HD : (h + 1) * HD] = whole[first : first + 64]


def attend(back, query, k_own, k_oth, v_own, v_oth, num, den):
    args = [query, k_own, k_oth, v_own, v_oth]
    aliases = {}
    outs = [
        jax.ShapeDtypeStruct((4, 512, HD), jnp.float32),
        jax.ShapeDtypeStruct((4, 512, HALF), jnp.float32),
    ]
    out_specs = [vspec(), vspec()]
    if back:
        args += [num, den]
    if back == 1:
        aliases = {5: 0, 6: 1}
    if back == 2:
        outs = jax.ShapeDtypeStruct((4, 4, 64, 512), jnp.bfloat16)
        out_specs = vspec()
    pairs = {0: 20, 1: 32, 2: 20}[back]
    return pl.pallas_call(
        functools.partial(attend_kernel, back),
        out_shape=outs,
        in_specs=[vspec()] * len(args),
        out_specs=out_specs,
        input_output_aliases=aliases,
        compiler_params=pltpu.CompilerParams(vmem_limit_bytes=24 << 20),
        cost_estimate=pl.CostEstimate(
            flops=int(pairs * 512 * 256 * 256 * 4 * 0.2),
            bytes_accessed=1 << 16,
            transcendentals=1,
        ),
        name="attend_%d" % back,
    )(*args)


def combine_kernel(got_ref, res_ref, g0_ref, g1_ref, g2_ref, g3_ref, out_ref, gain_ref):
    section = lax.axis_index("section")
    for r, ref in enumerate((g0_ref, g1_ref, g2_ref, g3_ref)):
        gain_ref[pl.ds(lax.rem(section + 4 - r, 4), 1), :] = ref[...]
    rows = pl.ds(pl.multiple_of(section * 64, 64), 64)
    running = res_ref[rows, :].astype(jnp.float32)
    running = [running[:, h * 512 : (h + 1) * 512] for h in range(4)]
    for layer in range(LAYERS):
        parts = [got_ref[layer * 4 + h].astype(jnp.float32) for h in range(4)]
        square = sum(jnp.sum(p * p, axis=-1, keepdims=True) for p in parts)
        norm = lax.rsqrt(square * (1.0 / (HQ * HD)) + 1e-06)
        for h in range(4):
            gain = gain_ref[layer : layer + 1, h * 512 : (h + 1) * 512]
            running[h] = running[h] + parts[h] * norm * gain
            out_ref[layer, :, h * 512 : (h + 1) * 512] = running[h].astype(jnp.bfloat16)


def per_device(queries, keys, values, segment_ids, positions, residual_in, post_gain):
    inverse = jnp.exp(-math.log(10000.0) * jnp.arange(HALF).astype(jnp.float32) / HALF)
    angle = positions.astype(jnp.float32)[:, None] * inverse[None, :]
    cosine = jnp.cos(angle)
    sine = jnp.sin(angle)
    split = jnp.stack([lax.shift_right_logical(positions, 7), positions & 127])
    places = jnp.concatenate([split, jnp.zeros((14, ROWS), jnp.int32)]).astype(jnp.bfloat16)

    def over_y(x):
        return lax.all_to_all(x, "seq", 0, 0, axis_index_groups=SHARED_Y)

    def onward(x):
        return lax.ppermute(x, "seq", NEXT_PLANE)

    def other(x):
        return lax.ppermute(x, "seq", OTHER_CORE)

    gains = [post_gain] + [
        lax.ppermute(post_gain, "section", [(i, (i + r) % 4) for i in range(4)])
        for r in (1, 2, 3)
    ]
    v_msg = pl.pallas_call(
        split_v_kernel,
        out_shape=jax.ShapeDtypeStruct((HK, ROWS, HD), jnp.bfloat16),
        in_specs=[vspec()],
        out_specs=vspec(),
        name="split_v",
    )(values[0])
    k_msg = pl.pallas_call(
        rotate_k_kernel,
        out_shape=jax.ShapeDtypeStruct((HK, ROWS, HD), jnp.bfloat16),
        in_specs=[vspec()] * 3,
        out_specs=vspec(),
        name="rotate_k",
    )(cosine, sine, keys[0])
    q_msg = pl.pallas_call(
        rotate_q_kernel,
        out_shape=jax.ShapeDtypeStruct((HK, 2 * ROWS + 16, HD), jnp.bfloat16),
        in_specs=[vspec()] * 4,
        out_specs=vspec(),
        name="rotate_q",
    )(cosine, sine, places, queries[0])

    v0 = over_y(v_msg)
    v0, k_msg = lax.optimization_barrier((v0, k_msg))
    v1 = onward(v0)
    k0 = over_y(k_msg)
    k1 = onward(k0)
    v1, q_msg = lax.optimization_barrier((v1, q_msg))
    query = over_y(q_msg)
    v2 = onward(v1)
    k2 = onward(k1)

    num, den = attend(0, query, k0, other(k0), v0, other(v0), None, None)
    num, den, v2 = lax.optimization_barrier((num, den, v2))
    num, den = attend(1, query, k1, other(k1), v1, other(v1), num, den)
    num, den, k2 = lax.optimization_barrier((num, den, k2))
    sent = attend(2, query, k2, other(k2), v2, other(v2), num, den)
    got = lax.all_to_all(
        sent.reshape(16, 64, 512), ("section", "seq"), 0, 0, axis_index_groups=SHARED_XY
    )
    back = pl.pallas_call(
        combine_kernel,
        out_shape=jax.ShapeDtypeStruct((LAYERS, 64, HQ * HD), jnp.bfloat16),
        in_specs=[vspec()] * 6,
        out_specs=vspec(),
        scratch_shapes=[VMEM((LAYERS, HQ * HD), jnp.float32)],
        name="combine",
    )(got, residual_in, *gains)
    mine = lax.all_to_all(back, "section", 0, 0)
    return mine.reshape(1, ROWS, HQ * HD)


def solution(mesh):
    placed = (
        P("section", "seq", None),
        P("section", "seq", None),
        P("section", "seq", None),
        P("seq"),
        P("seq"),
        P("seq", None),
        P("section", None),
    )
    return jax.shard_map(
        per_device, mesh=mesh, in_specs=placed, out_specs=P("section", "seq", None), check_vma=False
    )
```

```python
import functools
import math

import jax
import jax.numpy as jnp
from jax import lax
from jax.experimental import pallas as pl
from jax.experimental.pallas import tpu as pltpu
from jax.sharding import PartitionSpec as P

HQ = 8
HK = 4
HD = 256
WINDOW = 4096
ROWS = 256
PLANE = 2048
LAYERS = 4
HALF = HD // 2
VMEM = pltpu.VMEM
CAP = 50.0 / math.log(2.0)

SHARED_Y = [[z * 8 + y * 2 + c for y in range(4)] for z in range(8) for c in range(2)]
SHARED_XY = [
    [x * 64 + z * 8 + y * 2 + c for x in range(4) for y in range(4)]
    for z in range(8)
    for c in range(2)
]
NEXT_PLANE = [(i, i + 8) for i in range(56)]
OTHER_CORE = [(i, i ^ 1) for i in range(64)]


def vspec():
    return pl.BlockSpec(memory_space=VMEM)


def turned(x, cosine, sine):
    first = x[:, :HALF].astype(jnp.float32)
    second = x[:, HALF:].astype(jnp.float32)
    return (
        (first * cosine - second * sine).astype(jnp.bfloat16),
        (second * cosine + first * sine).astype(jnp.bfloat16),
    )


def split_v_kernel(v_ref, vm_ref):
    for h in range(HK):
        vm_ref[h] = v_ref[:, h * HD : (h + 1) * HD]


def rotate_k_kernel(cos_ref, sin_ref, k_ref, km_ref):
    for h in range(HK):
        a, b = turned(k_ref[:, h * HD : (h + 1) * HD], cos_ref[...], sin_ref[...])
        km_ref[h, :, :HALF] = a
        km_ref[h, :, HALF:] = b


def rotate_q_kernel(cos_ref, sin_ref, place_ref, q_ref, qm_ref):
    for h in range(HQ):
        a, b = turned(q_ref[:, h * HD : (h + 1) * HD], cos_ref[...], sin_ref[...])
        rows = pl.ds((h % 2) * ROWS, ROWS)
        qm_ref[h // 2, rows, :HALF] = a
        qm_ref[h // 2, rows, HALF:] = b
    for h in range(HK):
        qm_ref[h, 2 * ROWS :] = place_ref[...]


def attend_kernel(back, q_ref, k_own, k_oth, v_own, v_oth, *refs):
    if back == 0:
        num, den = refs
    elif back == 1:
        num_in, den_in, num, den = refs
    else:
        num_in, den_in, out_ref = refs
    device = lax.axis_index("seq")
    plane0 = device // 8 * PLANE
    core = lax.rem(device, 2)
    keys0 = plane0 - back * PLANE
    for r in range(4):
        begin, end = {0: (0, r + 1), 1: (0, 4), 2: (r, 4)}[back]
        count = (end - begin) * ROWS
        query = q_ref[r, : 2 * ROWS]
        split = q_ref[r, 2 * ROWS :].astype(jnp.float32)
        place = (split[0:1] * 128.0 + split[1:2]).astype(jnp.int32)
        token = plane0 + r * 512 + core * ROWS + lax.broadcasted_iota(jnp.int32, (1, ROWS), 1)
        low = token - jnp.minimum(place, WINDOW - 1)
        low = jnp.transpose(jnp.broadcast_to(low, (HALF, ROWS)))
        low = jnp.concatenate([low, low], axis=0)
        low = jnp.concatenate([low] * (count // HALF), axis=1)
        col = lax.broadcasted_iota(jnp.int32, (1, count), 1)
        spread = col + lax.shift_right_logical(col, 8) * ROWS + begin * 512 + keys0
        total, added = None, None
        for k_ref, v_ref, side in ((k_own, v_own, core), (k_oth, v_oth, 1 - core)):
            score = lax.dot_general(
                query,
                k_ref[begin:end].reshape(count, HD),
                (((1,), (1,)), ((), ())),
                preferred_element_type=jnp.float32,
            )
            weight = jnp.exp2(jnp.tanh(score * (1.0 / 800.0)) * CAP)
            key = spread + side * ROWS
            ok = key >= low
            if back == 0:
                row = lax.broadcasted_iota(jnp.int32, (2 * ROWS, 1), 0) & (ROWS - 1)
                ok = ok & (key <= plane0 + r * 512 + core * ROWS + row)
            weight = jnp.where(ok, weight, 0.0)
            lanes = sum(weight[:, i * HALF : (i + 1) * HALF] for i in range(count // HALF))
            part = jnp.dot(
                weight.astype(jnp.bfloat16),
                v_ref[begin:end].reshape(count, HD),
                preferred_element_type=jnp.float32,
            )
            total = lanes if total is None else total + lanes
            added = part if added is None else added + part
        if back == 0:
            num[r] = added
            den[r] = total
        elif back == 1:
            num[r] = num_in[r] + added
            den[r] = den_in[r] + total
        else:
            scale = 1.0 / jnp.sum(den_in[r] + total, axis=-1, keepdims=True)
            whole = ((num_in[r] + added) * scale).astype(jnp.bfloat16)
            for q in range(4):
                for h in range(2):
                    first = h * ROWS + q * 64
                    out_ref[q, r, :, h * HD : (h + 1) * HD] = whole[first : first + 64]


def attend(back, query, k_own, k_oth, v_own, v_oth, num, den):
    args = [query, k_own, k_oth, v_own, v_oth]
    aliases = {}
    outs = [
        jax.ShapeDtypeStruct((4, 512, HD), jnp.float32),
        jax.ShapeDtypeStruct((4, 512, HALF), jnp.float32),
    ]
    out_specs = [vspec(), vspec()]
    if back:
        args += [num, den]
    if back == 1:
        aliases = {5: 0, 6: 1}
    if back == 2:
        outs = jax.ShapeDtypeStruct((4, 4, 64, 512), jnp.bfloat16)
        out_specs = vspec()
    pairs = {0: 20, 1: 32, 2: 20}[back]
    return pl.pallas_call(
        functools.partial(attend_kernel, back),
        out_shape=outs,
        in_specs=[vspec()] * len(args),
        out_specs=out_specs,
        input_output_aliases=aliases,
        compiler_params=pltpu.CompilerParams(vmem_limit_bytes=24 << 20),
        cost_estimate=pl.CostEstimate(
            flops=int(pairs * 512 * 256 * 256 * 4 * 0.2),
            bytes_accessed=1 << 16,
            transcendentals=1,
        ),
        name="attend_%d" % back,
    )(*args)


def combine_kernel(got_ref, res_ref, g0_ref, g1_ref, g2_ref, g3_ref, out_ref, gain_ref):
    section = lax.axis_index("section")
    for r, ref in enumerate((g0_ref, g1_ref, g2_ref, g3_ref)):
        gain_ref[pl.ds(lax.rem(section + 4 - r, 4), 1), :] = ref[...]
    running = res_ref[...].astype(jnp.float32)
    running = [running[:, h * 512 : (h + 1) * 512] for h in range(4)]
    for layer in range(LAYERS):
        parts = [got_ref[layer * 4 + h].astype(jnp.float32) for h in range(4)]
        square = sum(jnp.sum(p * p, axis=-1, keepdims=True) for p in parts)
        norm = lax.rsqrt(square * (1.0 / (HQ * HD)) + 1e-06)
        for h in range(4):
            gain = gain_ref[layer : layer + 1, h * 512 : (h + 1) * 512]
            running[h] = running[h] + parts[h] * norm * gain
            out_ref[layer, :, h * 512 : (h + 1) * 512] = running[h].astype(jnp.bfloat16)


def per_device(queries, keys, values, segment_ids, positions, residual_in, post_gain):
    inverse = jnp.exp(-math.log(10000.0) * jnp.arange(HALF).astype(jnp.float32) / HALF)
    angle = positions.astype(jnp.float32)[:, None] * inverse[None, :]
    cosine = jnp.cos(angle)
    sine = jnp.sin(angle)
    split = jnp.stack([lax.shift_right_logical(positions, 7), positions & 127])
    places = jnp.concatenate([split, jnp.zeros((14, ROWS), jnp.int32)]).astype(jnp.bfloat16)

    def over_y(x):
        return lax.all_to_all(x, "seq", 0, 0, axis_index_groups=SHARED_Y)

    def onward(x):
        return lax.ppermute(x, "seq", NEXT_PLANE)

    def other(x):
        return lax.ppermute(x, "seq", OTHER_CORE)

    gains = [post_gain] + [
        lax.ppermute(post_gain, "section", [(i, (i + r) % 4) for i in range(4)])
        for r in (1, 2, 3)
    ]
    v_msg = pl.pallas_call(
        split_v_kernel,
        out_shape=jax.ShapeDtypeStruct((HK, ROWS, HD), jnp.bfloat16),
        in_specs=[vspec()],
        out_specs=vspec(),
        name="split_v",
    )(values[0])
    k_msg = pl.pallas_call(
        rotate_k_kernel,
        out_shape=jax.ShapeDtypeStruct((HK, ROWS, HD), jnp.bfloat16),
        in_specs=[vspec()] * 3,
        out_specs=vspec(),
        name="rotate_k",
    )(cosine, sine, keys[0])
    q_msg = pl.pallas_call(
        rotate_q_kernel,
        out_shape=jax.ShapeDtypeStruct((HK, 2 * ROWS + 16, HD), jnp.bfloat16),
        in_specs=[vspec()] * 4,
        out_specs=vspec(),
        name="rotate_q",
    )(cosine, sine, places, queries[0])

    residual = lax.dynamic_slice_in_dim(residual_in, lax.axis_index("section") * 64, 64, 0)
    v0 = over_y(v_msg)
    v0, k_msg = lax.optimization_barrier((v0, k_msg))
    v1 = onward(v0)
    k0 = over_y(k_msg)
    k1 = onward(k0)
    v1, q_msg = lax.optimization_barrier((v1, q_msg))
    query = over_y(q_msg)
    v2 = onward(v1)
    k2 = onward(k1)

    num, den = attend(0, query, k0, other(k0), v0, other(v0), None, None)
    num, den, v2 = lax.optimization_barrier((num, den, v2))
    num, den = attend(1, query, k1, other(k1), v1, other(v1), num, den)
    num, den, k2, residual, *gains = lax.optimization_barrier((num, den, k2, residual, *gains))
    sent = attend(2, query, k2, other(k2), v2, other(v2), num, den)
    got = lax.all_to_all(
        sent.reshape(16, 64, 512), ("section", "seq"), 0, 0, axis_index_groups=SHARED_XY
    )
    back = pl.pallas_call(
        combine_kernel,
        out_shape=jax.ShapeDtypeStruct((LAYERS, 64, HQ * HD), jnp.bfloat16),
        in_specs=[vspec()] * 6,
        out_specs=vspec(),
        scratch_shapes=[VMEM((LAYERS, HQ * HD), jnp.float32)],
        compiler_params=pltpu.CompilerParams(vmem_limit_bytes=12 << 20),
        name="combine",
    )(got, residual, *gains)
    mine = lax.all_to_all(back, "section", 0, 0)
    return mine.reshape(1, ROWS, HQ * HD)


def solution(mesh):
    placed = (
        P("section", "seq", None),
        P("section", "seq", None),
        P("section", "seq", None),
        P("seq"),
        P("seq"),
        P("seq", None),
        P("section", None),
    )
    return jax.shard_map(
        per_device, mesh=mesh, in_specs=placed, out_specs=P("section", "seq", None), check_vma=False
    )
```

```python
import functools
import math

import jax
import jax.numpy as jnp
from jax import lax
from jax.experimental import pallas as pl
from jax.experimental.pallas import tpu as pltpu
from jax.sharding import PartitionSpec as P

HQ = 8
HK = 4
HD = 256
WINDOW = 4096
ROWS = 256
PLANE = 2048
LAYERS = 4
HALF = HD // 2
VMEM = pltpu.VMEM
CAP = 50.0 / math.log(2.0)

SHARED_Y = [[z * 8 + y * 2 + c for y in range(4)] for z in range(8) for c in range(2)]
SHARED_XY = [
    [x * 64 + z * 8 + y * 2 + c for x in range(4) for y in range(4)]
    for z in range(8)
    for c in range(2)
]
NEXT_PLANE = [(i, i + 8) for i in range(56)]
OTHER_CORE = [(i, i ^ 1) for i in range(64)]


def vspec():
    return pl.BlockSpec(memory_space=VMEM)


def turned(x, cosine, sine):
    first = x[:, :HALF].astype(jnp.float32)
    second = x[:, HALF:].astype(jnp.float32)
    return (
        (first * cosine - second * sine).astype(jnp.bfloat16),
        (second * cosine + first * sine).astype(jnp.bfloat16),
    )


def split_v_kernel(v_ref, *out_refs):
    y = lax.rem(lax.axis_index("seq") // 2, 4)
    for i, out_ref in enumerate(out_refs):
        lanes = pl.ds(pl.multiple_of(lax.rem(y + i, 4) * HD, HD), HD)
        out_ref[...] = v_ref[:, lanes]


def order_v_kernel(v0_ref, v1_ref, v2_ref, v3_ref, out_ref):
    y = lax.rem(lax.axis_index("seq") // 2, 4)
    for i, ref in enumerate((v0_ref, v1_ref, v2_ref, v3_ref)):
        out_ref[lax.rem(y + 4 - i, 4)] = ref[...]


def rotate_k_kernel(cos_ref, sin_ref, k_ref, km_ref):
    for h in range(HK):
        a, b = turned(k_ref[:, h * HD : (h + 1) * HD], cos_ref[...], sin_ref[...])
        km_ref[h, :, :HALF] = a
        km_ref[h, :, HALF:] = b


def rotate_q_kernel(cos_ref, sin_ref, place_ref, q_ref, qm_ref):
    for h in range(HQ):
        a, b = turned(q_ref[:, h * HD : (h + 1) * HD], cos_ref[...], sin_ref[...])
        rows = pl.ds((h % 2) * ROWS, ROWS)
        qm_ref[h // 2, rows, :HALF] = a
        qm_ref[h // 2, rows, HALF:] = b
    for h in range(HK):
        qm_ref[h, 2 * ROWS :] = place_ref[...]


def attend_kernel(back, q_ref, k_own, k_oth, v_own, v_oth, *refs):
    if back == 0:
        num, den = refs
    elif back == 1:
        num_in, den_in, num, den = refs
    else:
        num_in, den_in, out_ref = refs
    device = lax.axis_index("seq")
    plane0 = device // 8 * PLANE
    core = lax.rem(device, 2)
    keys0 = plane0 - back * PLANE
    for r in range(4):
        begin, end = {0: (0, r + 1), 1: (0, 4), 2: (r, 4)}[back]
        count = (end - begin) * ROWS
        query = q_ref[r, : 2 * ROWS]
        split = q_ref[r, 2 * ROWS :].astype(jnp.float32)
        place = (split[0:1] * 128.0 + split[1:2]).astype(jnp.int32)
        token = plane0 + r * 512 + core * ROWS + lax.broadcasted_iota(jnp.int32, (1, ROWS), 1)
        low = token - jnp.minimum(place, WINDOW - 1)
        low = jnp.transpose(jnp.broadcast_to(low, (HALF, ROWS)))
        low = jnp.concatenate([low, low], axis=0)
        low = jnp.concatenate([low] * (count // HALF), axis=1)
        col = lax.broadcasted_iota(jnp.int32, (1, count), 1)
        spread = col + lax.shift_right_logical(col, 8) * ROWS + begin * 512 + keys0
        total, added = None, None
        for k_ref, v_ref, side in ((k_own, v_own, core), (k_oth, v_oth, 1 - core)):
            score = lax.dot_general(
                query,
                k_ref[begin:end].reshape(count, HD),
                (((1,), (1,)), ((), ())),
                preferred_element_type=jnp.float32,
            )
            weight = jnp.exp2(jnp.tanh(score * (1.0 / 800.0)) * CAP)
            key = spread + side * ROWS
            ok = key >= low
            if back == 0:
                row = lax.broadcasted_iota(jnp.int32, (2 * ROWS, 1), 0) & (ROWS - 1)
                ok = ok & (key <= plane0 + r * 512 + core * ROWS + row)
            weight = jnp.where(ok, weight, 0.0)
            lanes = sum(weight[:, i * HALF : (i + 1) * HALF] for i in range(count // HALF))
            part = jnp.dot(
                weight.astype(jnp.bfloat16),
                v_ref[begin:end].reshape(count, HD),
                preferred_element_type=jnp.float32,
            )
            total = lanes if total is None else total + lanes
            added = part if added is None else added + part
        if back == 0:
            num[r] = added
            den[r] = total
        elif back == 1:
            num[r] = num_in[r] + added
            den[r] = den_in[r] + total
        else:
            scale = 1.0 / jnp.sum(den_in[r] + total, axis=-1, keepdims=True)
            whole = ((num_in[r] + added) * scale).astype(jnp.bfloat16)
            for q in range(4):
                for h in range(2):
                    first = h * ROWS + q * 64
                    out_ref[q, r, :, h * HD : (h + 1) * HD] = whole[first : first + 64]


def attend(back, query, k_own, k_oth, v_own, v_oth, num, den):
    args = [query, k_own, k_oth, v_own, v_oth]
    aliases = {}
    outs = [
        jax.ShapeDtypeStruct((4, 512, HD), jnp.float32),
        jax.ShapeDtypeStruct((4, 512, HALF), jnp.float32),
    ]
    out_specs = [vspec(), vspec()]
    if back:
        args += [num, den]
    if back == 1:
        aliases = {5: 0, 6: 1}
    if back == 2:
        outs = jax.ShapeDtypeStruct((4, 4, 64, 512), jnp.bfloat16)
        out_specs = vspec()
    pairs = {0: 20, 1: 32, 2: 20}[back]
    return pl.pallas_call(
        functools.partial(attend_kernel, back),
        out_shape=outs,
        in_specs=[vspec()] * len(args),
        out_specs=out_specs,
        input_output_aliases=aliases,
        compiler_params=pltpu.CompilerParams(vmem_limit_bytes=24 << 20),
        cost_estimate=pl.CostEstimate(
            flops=int(pairs * 512 * 256 * 256 * 4 * 0.2),
            bytes_accessed=1 << 16,
            transcendentals=1,
        ),
        name="attend_%d" % back,
    )(*args)


def combine_kernel(got_ref, res_ref, g0_ref, g1_ref, g2_ref, g3_ref, out_ref, gain_ref):
    section = lax.axis_index("section")
    for r, ref in enumerate((g0_ref, g1_ref, g2_ref, g3_ref)):
        gain_ref[pl.ds(lax.rem(section + 4 - r, 4), 1), :] = ref[...]
    running = res_ref[...].astype(jnp.float32)
    running = [running[:, h * 512 : (h + 1) * 512] for h in range(4)]
    for layer in range(LAYERS):
        parts = [got_ref[layer * 4 + h].astype(jnp.float32) for h in range(4)]
        square = sum(jnp.sum(p * p, axis=-1, keepdims=True) for p in parts)
        norm = lax.rsqrt(square * (1.0 / (HQ * HD)) + 1e-06)
        for h in range(4):
            gain = gain_ref[layer : layer + 1, h * 512 : (h + 1) * 512]
            running[h] = running[h] + parts[h] * norm * gain
            out_ref[layer, :, h * 512 : (h + 1) * 512] = running[h].astype(jnp.bfloat16)


def per_device(queries, keys, values, segment_ids, positions, residual_in, post_gain):
    inverse = jnp.exp(-math.log(10000.0) * jnp.arange(HALF).astype(jnp.float32) / HALF)
    angle = positions.astype(jnp.float32)[:, None] * inverse[None, :]
    cosine = jnp.cos(angle)
    sine = jnp.sin(angle)
    split = jnp.stack([lax.shift_right_logical(positions, 7), positions & 127])
    places = jnp.concatenate([split, jnp.zeros((14, ROWS), jnp.int32)]).astype(jnp.bfloat16)

    def over_y(x):
        return lax.all_to_all(x, "seq", 0, 0, axis_index_groups=SHARED_Y)

    def onward(x):
        return lax.ppermute(x, "seq", NEXT_PLANE)

    def other(x):
        return lax.ppermute(x, "seq", OTHER_CORE)

    gains = [post_gain] + [
        lax.ppermute(post_gain, "section", [(i, (i + r) % 4) for i in range(4)])
        for r in (1, 2, 3)
    ]
    pieces = pl.pallas_call(
        split_v_kernel,
        out_shape=[jax.ShapeDtypeStruct((ROWS, HD), jnp.bfloat16)] * 4,
        in_specs=[vspec()],
        out_specs=[vspec()] * 4,
        name="split_v",
    )(values[0])
    pieces = [pieces[0]] + [
        lax.ppermute(pieces[i], "seq", [(d, d // 8 * 8 + (d + 2 * i) % 8) for d in range(64)])
        for i in (1, 2, 3)
    ]
    v0 = pl.pallas_call(
        order_v_kernel,
        out_shape=jax.ShapeDtypeStruct((HK, ROWS, HD), jnp.bfloat16),
        in_specs=[vspec()] * 4,
        out_specs=vspec(),
        compiler_params=pltpu.CompilerParams(vmem_limit_bytes=8 << 20),
        name="order_v",
    )(*pieces)
    k_msg = pl.pallas_call(
        rotate_k_kernel,
        out_shape=jax.ShapeDtypeStruct((HK, ROWS, HD), jnp.bfloat16),
        in_specs=[vspec()] * 3,
        out_specs=vspec(),
        name="rotate_k",
    )(cosine, sine, keys[0])
    q_msg = pl.pallas_call(
        rotate_q_kernel,
        out_shape=jax.ShapeDtypeStruct((HK, 2 * ROWS + 16, HD), jnp.bfloat16),
        in_specs=[vspec()] * 4,
        out_specs=vspec(),
        name="rotate_q",
    )(cosine, sine, places, queries[0])

    residual = lax.dynamic_slice_in_dim(residual_in, lax.axis_index("section") * 64, 64, 0)
    v1 = onward(v0)
    k0 = over_y(k_msg)
    k1 = onward(k0)
    v1, q_msg = lax.optimization_barrier((v1, q_msg))
    query = over_y(q_msg)
    v2 = onward(v1)
    k2 = onward(k1)

    num, den = attend(0, query, k0, other(k0), v0, other(v0), None, None)
    num, den, v2 = lax.optimization_barrier((num, den, v2))
    num, den = attend(1, query, k1, other(k1), v1, other(v1), num, den)
    num, den, k2, residual, *gains = lax.optimization_barrier((num, den, k2, residual, *gains))
    sent = attend(2, query, k2, other(k2), v2, other(v2), num, den)
    got = lax.all_to_all(
        sent.reshape(16, 64, 512), ("section", "seq"), 0, 0, axis_index_groups=SHARED_XY
    )
    back = pl.pallas_call(
        combine_kernel,
        out_shape=jax.ShapeDtypeStruct((LAYERS, 64, HQ * HD), jnp.bfloat16),
        in_specs=[vspec()] * 6,
        out_specs=vspec(),
        scratch_shapes=[VMEM((LAYERS, HQ * HD), jnp.float32)],
        compiler_params=pltpu.CompilerParams(vmem_limit_bytes=12 << 20),
        name="combine",
    )(got, residual, *gains)
    mine = lax.all_to_all(back, "section", 0, 0)
    return mine.reshape(1, ROWS, HQ * HD)


def solution(mesh):
    placed = (
        P("section", "seq", None),
        P("section", "seq", None),
        P("section", "seq", None),
        P("seq"),
        P("seq"),
        P("seq", None),
        P("section", None),
    )
    return jax.shard_map(
        per_device, mesh=mesh, in_specs=placed, out_specs=P("section", "seq", None), check_vma=False
    )
```

```python
import functools
import math

import jax
import jax.numpy as jnp
from jax import lax
from jax.experimental import pallas as pl
from jax.experimental.pallas import tpu as pltpu
from jax.sharding import PartitionSpec as P

HQ = 8
HK = 4
HD = 256
WINDOW = 4096
ROWS = 256
PLANE = 2048
LAYERS = 4
HALF = HD // 2
VMEM = pltpu.VMEM
CAP = 50.0 / math.log(2.0)

SHARED_Y = [[z * 8 + y * 2 + c for y in range(4)] for z in range(8) for c in range(2)]
SHARED_XY = [
    [x * 64 + z * 8 + y * 2 + c for x in range(4) for y in range(4)]
    for z in range(8)
    for c in range(2)
]
NEXT_PLANE = [(i, i + 8) for i in range(56)]
OTHER_CORE = [(i, i ^ 1) for i in range(64)]


def vspec():
    return pl.BlockSpec(memory_space=VMEM)


def turned(x, cosine, sine):
    first = x[:, :HALF].astype(jnp.float32)
    second = x[:, HALF:].astype(jnp.float32)
    return (
        (first * cosine - second * sine).astype(jnp.bfloat16),
        (second * cosine + first * sine).astype(jnp.bfloat16),
    )


def split_v_kernel(v_ref, *out_refs):
    y = lax.rem(lax.axis_index("seq") // 2, 4)
    for i, out_ref in enumerate(out_refs):
        lanes = pl.ds(pl.multiple_of(lax.rem(y + i, 4) * HD, HD), HD)
        out_ref[...] = v_ref[:, lanes]


def order_v_kernel(v0_ref, v1_ref, v2_ref, v3_ref, out_ref):
    y = lax.rem(lax.axis_index("seq") // 2, 4)
    for i, ref in enumerate((v0_ref, v1_ref, v2_ref, v3_ref)):
        out_ref[lax.rem(y + 4 - i, 4)] = ref[...]


def rotate_k_kernel(cos_ref, sin_ref, k_ref, km_ref):
    for h in range(HK):
        a, b = turned(k_ref[:, h * HD : (h + 1) * HD], cos_ref[...], sin_ref[...])
        km_ref[h, :, :HALF] = a
        km_ref[h, :, HALF:] = b


def rotate_q_kernel(cos_ref, sin_ref, place_ref, q_ref, qm_ref):
    for h in range(HQ):
        a, b = turned(q_ref[:, h * HD : (h + 1) * HD], cos_ref[...], sin_ref[...])
        rows = pl.ds((h % 2) * ROWS, ROWS)
        qm_ref[h // 2, rows, :HALF] = a
        qm_ref[h // 2, rows, HALF:] = b
    for h in range(HK):
        qm_ref[h, 2 * ROWS :] = place_ref[...]


def attend_kernel(back, q_ref, k_own, k_oth, v_own, v_oth, *refs):
    if back == 0:
        num, den = refs
    elif back == 1:
        num_in, den_in, num, den = refs
    else:
        num_in, den_in, out_ref = refs
    device = lax.axis_index("seq")
    plane0 = device // 8 * PLANE
    core = lax.rem(device, 2)
    keys0 = plane0 - back * PLANE
    for r in range(4):
        begin, end = {0: (0, r + 1), 1: (0, 4), 2: (r, 4)}[back]
        count = (end - begin) * ROWS
        query = q_ref[r, : 2 * ROWS]
        split = q_ref[r, 2 * ROWS :].astype(jnp.float32)
        place = (split[0:1] * 128.0 + split[1:2]).astype(jnp.int32)
        token = plane0 + r * 512 + core * ROWS + lax.broadcasted_iota(jnp.int32, (1, ROWS), 1)
        low = token - jnp.minimum(place, WINDOW - 1)
        low = jnp.transpose(jnp.broadcast_to(low, (HALF, ROWS)))
        low = jnp.concatenate([low, low], axis=0)
        low = jnp.concatenate([low] * (count // HALF), axis=1)
        col = lax.broadcasted_iota(jnp.int32, (1, count), 1)
        spread = col + lax.shift_right_logical(col, 8) * ROWS + begin * 512 + keys0
        total, added = None, None
        for k_ref, v_ref, side in ((k_own, v_own, core), (k_oth, v_oth, 1 - core)):
            score = lax.dot_general(
                query,
                k_ref[begin:end].reshape(count, HD),
                (((1,), (1,)), ((), ())),
                preferred_element_type=jnp.float32,
            )
            weight = jnp.exp2(jnp.tanh(score * (1.0 / 800.0)) * CAP)
            key = spread + side * ROWS
            ok = key >= low
            if back == 0:
                row = lax.broadcasted_iota(jnp.int32, (2 * ROWS, 1), 0) & (ROWS - 1)
                ok = ok & (key <= plane0 + r * 512 + core * ROWS + row)
            weight = jnp.where(ok, weight, 0.0)
            lanes = sum(weight[:, i * HALF : (i + 1) * HALF] for i in range(count // HALF))
            part = jnp.dot(
                weight.astype(jnp.bfloat16),
                v_ref[begin:end].reshape(count, HD),
                preferred_element_type=jnp.float32,
            )
            total = lanes if total is None else total + lanes
            added = part if added is None else added + part
        if back == 0:
            num[r] = added
            den[r] = total
        elif back == 1:
            num[r] = num_in[r] + added
            den[r] = den_in[r] + total
        else:
            scale = 1.0 / jnp.sum(den_in[r] + total, axis=-1, keepdims=True)
            whole = ((num_in[r] + added) * scale).astype(jnp.bfloat16)
            for q in range(4):
                for h in range(2):
                    first = h * ROWS + q * 64
                    out_ref[q, r, :, h * HD : (h + 1) * HD] = whole[first : first + 64]


def attend(back, query, k_own, k_oth, v_own, v_oth, num, den):
    args = [query, k_own, k_oth, v_own, v_oth]
    aliases = {}
    outs = [
        jax.ShapeDtypeStruct((4, 512, HD), jnp.float32),
        jax.ShapeDtypeStruct((4, 512, HALF), jnp.float32),
    ]
    out_specs = [vspec(), vspec()]
    if back:
        args += [num, den]
    if back == 1:
        aliases = {5: 0, 6: 1}
    if back == 2:
        outs = jax.ShapeDtypeStruct((4, 4, 64, 512), jnp.bfloat16)
        out_specs = vspec()
    pairs = {0: 20, 1: 32, 2: 20}[back]
    return pl.pallas_call(
        functools.partial(attend_kernel, back),
        out_shape=outs,
        in_specs=[vspec()] * len(args),
        out_specs=out_specs,
        input_output_aliases=aliases,
        compiler_params=pltpu.CompilerParams(vmem_limit_bytes=24 << 20),
        cost_estimate=pl.CostEstimate(
            flops=int(pairs * 512 * 256 * 256 * 4 * 0.2),
            bytes_accessed=1 << 16,
            transcendentals=1,
        ),
        name="attend_%d" % back,
    )(*args)


def combine_kernel(got_ref, res_ref, g0_ref, g1_ref, g2_ref, g3_ref, out_ref, gain_ref):
    section = lax.axis_index("section")
    for r, ref in enumerate((g0_ref, g1_ref, g2_ref, g3_ref)):
        gain_ref[pl.ds(lax.rem(section + 4 - r, 4), 1), :] = ref[...]
    running = res_ref[...].astype(jnp.float32)
    running = [running[:, h * 512 : (h + 1) * 512] for h in range(4)]
    for layer in range(LAYERS):
        parts = [got_ref[layer * 4 + h].astype(jnp.float32) for h in range(4)]
        square = sum(jnp.sum(p * p, axis=-1, keepdims=True) for p in parts)
        norm = lax.rsqrt(square * (1.0 / (HQ * HD)) + 1e-06)
        for h in range(4):
            gain = gain_ref[layer : layer + 1, h * 512 : (h + 1) * 512]
            running[h] = running[h] + parts[h] * norm * gain
            out_ref[layer, :, h * 512 : (h + 1) * 512] = running[h].astype(jnp.bfloat16)


def per_device(queries, keys, values, segment_ids, positions, residual_in, post_gain):
    inverse = jnp.exp(-math.log(10000.0) * jnp.arange(HALF).astype(jnp.float32) / HALF)
    angle = positions.astype(jnp.float32)[:, None] * inverse[None, :]
    cosine = jnp.cos(angle)
    sine = jnp.sin(angle)
    split = jnp.stack([lax.shift_right_logical(positions, 7), positions & 127])
    places = jnp.concatenate([split, jnp.zeros((14, ROWS), jnp.int32)]).astype(jnp.bfloat16)

    def over_y(x):
        return lax.all_to_all(x, "seq", 0, 0, axis_index_groups=SHARED_Y)

    def onward(x):
        return lax.ppermute(x, "seq", NEXT_PLANE)

    def other(x):
        return lax.ppermute(x, "seq", OTHER_CORE)

    gains = [post_gain] + [
        lax.ppermute(post_gain, "section", [(i, (i + r) % 4) for i in range(4)])
        for r in (1, 2, 3)
    ]
    pieces = pl.pallas_call(
        split_v_kernel,
        out_shape=[jax.ShapeDtypeStruct((ROWS, HD), jnp.bfloat16)] * 4,
        in_specs=[vspec()],
        out_specs=[vspec()] * 4,
        name="split_v",
    )(values[0])
    pieces = [pieces[0]] + [
        lax.ppermute(pieces[i], "seq", [(d, d // 8 * 8 + (d + 2 * i) % 8) for d in range(64)])
        for i in (1, 2, 3)
    ]
    v0 = pl.pallas_call(
        order_v_kernel,
        out_shape=jax.ShapeDtypeStruct((HK, ROWS, HD), jnp.bfloat16),
        in_specs=[vspec()] * 4,
        out_specs=vspec(),
        compiler_params=pltpu.CompilerParams(vmem_limit_bytes=8 << 20),
        name="order_v",
    )(*pieces)
    k_msg = pl.pallas_call(
        rotate_k_kernel,
        out_shape=jax.ShapeDtypeStruct((HK, ROWS, HD), jnp.bfloat16),
        in_specs=[vspec()] * 3,
        out_specs=vspec(),
        name="rotate_k",
    )(cosine, sine, keys[0])
    q_msg = pl.pallas_call(
        rotate_q_kernel,
        out_shape=jax.ShapeDtypeStruct((HK, 2 * ROWS + 16, HD), jnp.bfloat16),
        in_specs=[vspec()] * 4,
        out_specs=vspec(),
        name="rotate_q",
    )(cosine, sine, places, queries[0])

    residual = lax.dynamic_slice_in_dim(residual_in, lax.axis_index("section") * 64, 64, 0)
    v1 = onward(v0)
    k0 = over_y(k_msg)
    k0, q_msg = lax.optimization_barrier((k0, q_msg))
    k1 = onward(k0)
    v1, q_msg = lax.optimization_barrier((v1, q_msg))
    query = over_y(q_msg)
    v2 = onward(v1)
    k2 = onward(k1)
    num, den = attend(0, query, k0, other(k0), v0, other(v0), None, None)
    num, den, v2 = lax.optimization_barrier((num, den, v2))
    num, den = attend(1, query, k1, other(k1), v1, other(v1), num, den)
    num, den, k2, residual, *gains = lax.optimization_barrier((num, den, k2, residual, *gains))
    sent = attend(2, query, k2, other(k2), v2, other(v2), num, den)
    got = lax.all_to_all(
        sent.reshape(16, 64, 512), ("section", "seq"), 0, 0, axis_index_groups=SHARED_XY
    )
    back = pl.pallas_call(
        combine_kernel,
        out_shape=jax.ShapeDtypeStruct((LAYERS, 64, HQ * HD), jnp.bfloat16),
        in_specs=[vspec()] * 6,
        out_specs=vspec(),
        scratch_shapes=[VMEM((LAYERS, HQ * HD), jnp.float32)],
        compiler_params=pltpu.CompilerParams(vmem_limit_bytes=12 << 20),
        name="combine",
    )(got, residual, *gains)
    mine = lax.all_to_all(back, "section", 0, 0)
    return mine.reshape(1, ROWS, HQ * HD)


def solution(mesh):
    placed = (
        P("section", "seq", None),
        P("section", "seq", None),
        P("section", "seq", None),
        P("seq"),
        P("seq"),
        P("seq", None),
        P("section", None),
    )
    return jax.shard_map(
        per_device, mesh=mesh, in_specs=placed, out_specs=P("section", "seq", None), check_vma=False
    )
```

```python
import functools
import math

import jax
import jax.numpy as jnp
from jax import lax
from jax.experimental import pallas as pl
from jax.experimental.pallas import tpu as pltpu
from jax.sharding import PartitionSpec as P

HQ = 8
HK = 4
HD = 256
WINDOW = 4096
ROWS = 256
PLANE = 2048
LAYERS = 4
HALF = HD // 2
VMEM = pltpu.VMEM
CAP = 50.0 / math.log(2.0)

SHARED_Y = [[z * 8 + y * 2 + c for y in range(4)] for z in range(8) for c in range(2)]
SHARED_XY = [
    [x * 64 + z * 8 + y * 2 + c for x in range(4) for y in range(4)]
    for z in range(8)
    for c in range(2)
]
NEXT_PLANE = [(i, i + 8) for i in range(56)]
OTHER_CORE = [(i, i ^ 1) for i in range(64)]


def vspec():
    return pl.BlockSpec(memory_space=VMEM)


def turned(x, cosine, sine):
    first = x[:, :HALF].astype(jnp.float32)
    second = x[:, HALF:].astype(jnp.float32)
    return (
        (first * cosine - second * sine).astype(jnp.bfloat16),
        (second * cosine + first * sine).astype(jnp.bfloat16),
    )


def split_v_kernel(v_ref, *out_refs):
    y = lax.rem(lax.axis_index("seq") // 2, 4)
    for i, out_ref in enumerate(out_refs):
        lanes = pl.ds(pl.multiple_of(lax.rem(y + i, 4) * HD, HD), HD)
        out_ref[...] = v_ref[:, lanes]


def order_v_kernel(v0_ref, v1_ref, v2_ref, v3_ref, out_ref):
    y = lax.rem(lax.axis_index("seq") // 2, 4)
    for i, ref in enumerate((v0_ref, v1_ref, v2_ref, v3_ref)):
        out_ref[lax.rem(y + 4 - i, 4)] = ref[...]


def rotate_k_kernel(cos_ref, sin_ref, k_ref, km_ref):
    for h in range(HK):
        a, b = turned(k_ref[:, h * HD : (h + 1) * HD], cos_ref[...], sin_ref[...])
        km_ref[h, :, :HALF] = a
        km_ref[h, :, HALF:] = b


def rotate_q_kernel(cos_ref, sin_ref, place_ref, q_ref, qm_ref):
    for h in range(HQ):
        a, b = turned(q_ref[:, h * HD : (h + 1) * HD], cos_ref[...], sin_ref[...])
        rows = pl.ds((h % 2) * ROWS, ROWS)
        qm_ref[h // 2, rows, :HALF] = a
        qm_ref[h // 2, rows, HALF:] = b
    for h in range(HK):
        qm_ref[h, 2 * ROWS :] = place_ref[...]


def attend_kernel(last, q_ref, *refs):
    if last:
        planes = ((2, refs[:4]),)
        num_in, den_in, out_ref = refs[4:]
    else:
        planes = ((1, refs[4:8]), (0, refs[:4]))
        num, den = refs[8:]
    device = lax.axis_index("seq")
    plane0 = device // 8 * PLANE
    core = lax.rem(device, 2)
    for r in range(4):
        query = q_ref[r, : 2 * ROWS]
        split = q_ref[r, 2 * ROWS :].astype(jnp.float32)
        place = (split[0:1] * 128.0 + split[1:2]).astype(jnp.int32)
        token = plane0 + r * 512 + core * ROWS + lax.broadcasted_iota(jnp.int32, (1, ROWS), 1)
        first = token - jnp.minimum(place, WINDOW - 1)
        first = jnp.transpose(jnp.broadcast_to(first, (HALF, ROWS)))
        first = jnp.concatenate([first, first], axis=0)
        total, added = None, None
        for back, (k_own, k_oth, v_own, v_oth) in planes:
            begin, end = {0: (0, r + 1), 1: (0, 4), 2: (r, 4)}[back]
            count = (end - begin) * ROWS
            low = jnp.concatenate([first] * (count // HALF), axis=1)
            col = lax.broadcasted_iota(jnp.int32, (1, count), 1)
            spread = col + lax.shift_right_logical(col, 8) * ROWS + begin * 512
            spread = spread + plane0 - back * PLANE
            for k_ref, v_ref, side in ((k_own, v_own, core), (k_oth, v_oth, 1 - core)):
                score = lax.dot_general(
                    query,
                    k_ref[begin:end].reshape(count, HD),
                    (((1,), (1,)), ((), ())),
                    preferred_element_type=jnp.float32,
                )
                weight = jnp.exp2(jnp.tanh(score * (1.0 / 800.0)) * CAP)
                key = spread + side * ROWS
                ok = key >= low
                if back == 0:
                    row = lax.broadcasted_iota(jnp.int32, (2 * ROWS, 1), 0) & (ROWS - 1)
                    ok = ok & (key <= plane0 + r * 512 + core * ROWS + row)
                weight = jnp.where(ok, weight, 0.0)
                lanes = sum(weight[:, i * HALF : (i + 1) * HALF] for i in range(count // HALF))
                part = jnp.dot(
                    weight.astype(jnp.bfloat16),
                    v_ref[begin:end].reshape(count, HD),
                    preferred_element_type=jnp.float32,
                )
                total = lanes if total is None else total + lanes
                added = part if added is None else added + part
        if last:
            scale = 1.0 / jnp.sum(den_in[r] + total, axis=-1, keepdims=True)
            whole = ((num_in[r] + added) * scale).astype(jnp.bfloat16)
            for q in range(4):
                for h in range(2):
                    top = h * ROWS + q * 64
                    out_ref[q, r, :, h * HD : (h + 1) * HD] = whole[top : top + 64]
        else:
            num[r] = added
            den[r] = total


def attend(last, query, *args):
    outs = [
        jax.ShapeDtypeStruct((4, 512, HD), jnp.float32),
        jax.ShapeDtypeStruct((4, 512, HALF), jnp.float32),
    ]
    out_specs = [vspec(), vspec()]
    if last:
        outs = jax.ShapeDtypeStruct((4, 4, 64, 512), jnp.bfloat16)
        out_specs = vspec()
    return pl.pallas_call(
        functools.partial(attend_kernel, last),
        out_shape=outs,
        in_specs=[vspec()] * (1 + len(args)),
        out_specs=out_specs,
        compiler_params=pltpu.CompilerParams(vmem_limit_bytes=24 << 20),
        cost_estimate=pl.CostEstimate(
            flops=20 * 512 * 256 * 256, bytes_accessed=1 << 16, transcendentals=1
        ),
        name="attend_last" if last else "attend_near",
    )(query, *args)


def combine_kernel(got_ref, res_ref, g0_ref, g1_ref, g2_ref, g3_ref, out_ref, gain_ref):
    section = lax.axis_index("section")
    for r, ref in enumerate((g0_ref, g1_ref, g2_ref, g3_ref)):
        gain_ref[pl.ds(lax.rem(section + 4 - r, 4), 1), :] = ref[...]
    running = res_ref[...].astype(jnp.float32)
    running = [running[:, h * 512 : (h + 1) * 512] for h in range(4)]
    for layer in range(LAYERS):
        parts = [got_ref[layer * 4 + h].astype(jnp.float32) for h in range(4)]
        square = sum(jnp.sum(p * p, axis=-1, keepdims=True) for p in parts)
        norm = lax.rsqrt(square * (1.0 / (HQ * HD)) + 1e-06)
        for h in range(4):
            gain = gain_ref[layer : layer + 1, h * 512 : (h + 1) * 512]
            running[h] = running[h] + parts[h] * norm * gain
            out_ref[layer, :, h * 512 : (h + 1) * 512] = running[h].astype(jnp.bfloat16)


def per_device(queries, keys, values, segment_ids, positions, residual_in, post_gain):
    inverse = jnp.exp(-math.log(10000.0) * jnp.arange(HALF).astype(jnp.float32) / HALF)
    angle = positions.astype(jnp.float32)[:, None] * inverse[None, :]
    cosine = jnp.cos(angle)
    sine = jnp.sin(angle)
    later, values = lax.optimization_barrier((positions, values))
    split = jnp.stack([lax.shift_right_logical(later, 7), later & 127])
    places = jnp.concatenate([split, jnp.zeros((14, ROWS), jnp.int32)]).astype(jnp.bfloat16)

    def over_y(x):
        return lax.all_to_all(x, "seq", 0, 0, axis_index_groups=SHARED_Y)

    def onward(x):
        return lax.ppermute(x, "seq", NEXT_PLANE)

    def other(x):
        return lax.ppermute(x, "seq", OTHER_CORE)

    gains = [post_gain] + [
        lax.ppermute(post_gain, "section", [(i, (i + r) % 4) for i in range(4)])
        for r in (1, 2, 3)
    ]
    pieces = pl.pallas_call(
        split_v_kernel,
        out_shape=[jax.ShapeDtypeStruct((ROWS, HD), jnp.bfloat16)] * 4,
        in_specs=[vspec()],
        out_specs=[vspec()] * 4,
        name="split_v",
    )(values[0])
    pieces = [pieces[0]] + [
        lax.ppermute(pieces[i], "seq", [(d, d // 8 * 8 + (d + 2 * i) % 8) for d in range(64)])
        for i in (1, 2, 3)
    ]
    v0 = pl.pallas_call(
        order_v_kernel,
        out_shape=jax.ShapeDtypeStruct((HK, ROWS, HD), jnp.bfloat16),
        in_specs=[vspec()] * 4,
        out_specs=vspec(),
        compiler_params=pltpu.CompilerParams(vmem_limit_bytes=8 << 20),
        name="order_v",
    )(*pieces)
    k_msg = pl.pallas_call(
        rotate_k_kernel,
        out_shape=jax.ShapeDtypeStruct((HK, ROWS, HD), jnp.bfloat16),
        in_specs=[vspec()] * 3,
        out_specs=vspec(),
        name="rotate_k",
    )(cosine, sine, keys[0])
    q_msg = pl.pallas_call(
        rotate_q_kernel,
        out_shape=jax.ShapeDtypeStruct((HK, 2 * ROWS + 16, HD), jnp.bfloat16),
        in_specs=[vspec()] * 4,
        out_specs=vspec(),
        name="rotate_q",
    )(cosine, sine, places, queries[0])

    residual = lax.dynamic_slice_in_dim(residual_in, lax.axis_index("section") * 64, 64, 0)
    v1 = onward(v0)
    k0 = over_y(k_msg)
    k0, q_msg = lax.optimization_barrier((k0, q_msg))
    k1 = onward(k0)
    v1, q_msg = lax.optimization_barrier((v1, q_msg))
    query = over_y(q_msg)
    v2 = onward(v1)
    k2 = onward(k1)
    num, den = attend(
        False, query, k0, other(k0), v0, other(v0), k1, other(k1), v1, other(v1)
    )
    num, den, k2, residual, *gains = lax.optimization_barrier((num, den, k2, residual, *gains))
    sent = attend(True, query, k2, other(k2), v2, other(v2), num, den)
    got = lax.all_to_all(
        sent.reshape(16, 64, 512), ("section", "seq"), 0, 0, axis_index_groups=SHARED_XY
    )
    back = pl.pallas_call(
        combine_kernel,
        out_shape=jax.ShapeDtypeStruct((LAYERS, 64, HQ * HD), jnp.bfloat16),
        in_specs=[vspec()] * 6,
        out_specs=vspec(),
        scratch_shapes=[VMEM((LAYERS, HQ * HD), jnp.float32)],
        compiler_params=pltpu.CompilerParams(vmem_limit_bytes=12 << 20),
        name="combine",
    )(got, residual, *gains)
    mine = lax.all_to_all(back, "section", 0, 0)
    return mine.reshape(1, ROWS, HQ * HD)


def solution(mesh):
    placed = (
        P("section", "seq", None),
        P("section", "seq", None),
        P("section", "seq", None),
        P("seq"),
        P("seq"),
        P("seq", None),
        P("section", None),
    )
    return jax.shard_map(
        per_device, mesh=mesh, in_specs=placed, out_specs=P("section", "seq", None), check_vma=False
    )
```

```python
import functools
import math

import jax
import jax.numpy as jnp
from jax import lax
from jax.experimental import pallas as pl
from jax.experimental.pallas import tpu as pltpu
from jax.sharding import PartitionSpec as P

HQ = 8
HK = 4
HD = 256
WINDOW = 4096
ROWS = 256
PLANE = 2048
LAYERS = 4
HALF = HD // 2
VMEM = pltpu.VMEM
CAP = 50.0 / math.log(2.0)

SHARED_Y = [[z * 8 + y * 2 + c for y in range(4)] for z in range(8) for c in range(2)]
SHARED_XY = [
    [x * 64 + z * 8 + y * 2 + c for x in range(4) for y in range(4)]
    for z in range(8)
    for c in range(2)
]
NEXT_PLANE = [(i, i + 8) for i in range(56)]
OTHER_CORE = [(i, i ^ 1) for i in range(64)]


def vspec():
    return pl.BlockSpec(memory_space=VMEM)


def turned(x, cosine, sine):
    first = x[:, :HALF].astype(jnp.float32)
    second = x[:, HALF:].astype(jnp.float32)
    return (
        (first * cosine - second * sine).astype(jnp.bfloat16),
        (second * cosine + first * sine).astype(jnp.bfloat16),
    )


def split_v_kernel(v_ref, *out_refs):
    y = lax.rem(lax.axis_index("seq") // 2, 4)
    for i, out_ref in enumerate(out_refs):
        lanes = pl.ds(pl.multiple_of(lax.rem(y + i, 4) * HD, HD), HD)
        out_ref[...] = v_ref[:, lanes]


def order_v_kernel(v0_ref, v1_ref, v2_ref, v3_ref, out_ref):
    y = lax.rem(lax.axis_index("seq") // 2, 4)
    for i, ref in enumerate((v0_ref, v1_ref, v2_ref, v3_ref)):
        out_ref[lax.rem(y + 4 - i, 4)] = ref[...]


def rotate_k_kernel(cos_ref, sin_ref, k_ref, km_ref):
    for h in range(HK):
        a, b = turned(k_ref[:, h * HD : (h + 1) * HD], cos_ref[...], sin_ref[...])
        km_ref[h, :, :HALF] = a
        km_ref[h, :, HALF:] = b


def rotate_q_kernel(cos_ref, sin_ref, place_ref, q_ref, qm_ref):
    for h in range(HQ):
        a, b = turned(q_ref[:, h * HD : (h + 1) * HD], cos_ref[...], sin_ref[...])
        rows = pl.ds((h % 2) * ROWS, ROWS)
        qm_ref[h // 2, rows, :HALF] = a
        qm_ref[h // 2, rows, HALF:] = b
    for h in range(HK):
        qm_ref[h, 2 * ROWS :] = place_ref[...]


def attend_kernel(back, part, q_ref, *refs):
    device = lax.axis_index("seq")
    plane0 = device // 8 * PLANE
    core = lax.rem(device, 2)
    if part == "both":
        pairs = ((refs[0], refs[2], core), (refs[1], refs[3], 1 - core))
        refs = refs[4:]
    else:
        pairs = ((refs[0], refs[1], core if part == "own" else 1 - core),)
        refs = refs[2:]
    last = part == "other"
    if back == 0:
        num, den = refs
    elif last:
        num_in, den_in, out_ref = refs
    else:
        num_in, den_in, num, den = refs
    keys0 = plane0 - back * PLANE
    for r in range(4):
        begin, end = {0: (0, r + 1), 1: (0, 4), 2: (r, 4)}[back]
        count = (end - begin) * ROWS
        query = q_ref[r, : 2 * ROWS]
        split = q_ref[r, 2 * ROWS :].astype(jnp.float32)
        place = (split[0:1] * 128.0 + split[1:2]).astype(jnp.int32)
        token = plane0 + r * 512 + core * ROWS + lax.broadcasted_iota(jnp.int32, (1, ROWS), 1)
        low = token - jnp.minimum(place, WINDOW - 1)
        low = jnp.transpose(jnp.broadcast_to(low, (HALF, ROWS)))
        low = jnp.concatenate([low, low], axis=0)
        low = jnp.concatenate([low] * (count // HALF), axis=1)
        col = lax.broadcasted_iota(jnp.int32, (1, count), 1)
        spread = col + lax.shift_right_logical(col, 8) * ROWS + begin * 512 + keys0
        total, added = None, None
        for k_ref, v_ref, side in pairs:
            score = lax.dot_general(
                query,
                k_ref[begin:end].reshape(count, HD),
                (((1,), (1,)), ((), ())),
                preferred_element_type=jnp.float32,
            )
            weight = jnp.exp2(jnp.tanh(score * (1.0 / 800.0)) * CAP)
            key = spread + side * ROWS
            ok = key >= low
            if back == 0:
                row = lax.broadcasted_iota(jnp.int32, (2 * ROWS, 1), 0) & (ROWS - 1)
                ok = ok & (key <= plane0 + r * 512 + core * ROWS + row)
            weight = jnp.where(ok, weight, 0.0)
            lanes = sum(weight[:, i * HALF : (i + 1) * HALF] for i in range(count // HALF))
            part = jnp.dot(
                weight.astype(jnp.bfloat16),
                v_ref[begin:end].reshape(count, HD),
                preferred_element_type=jnp.float32,
            )
            total = lanes if total is None else total + lanes
            added = part if added is None else added + part
        if back == 0:
            num[r] = added
            den[r] = total
        elif not last:
            num[r] = num_in[r] + added
            den[r] = den_in[r] + total
        else:
            scale = 1.0 / jnp.sum(den_in[r] + total, axis=-1, keepdims=True)
            whole = ((num_in[r] + added) * scale).astype(jnp.bfloat16)
            for q in range(4):
                for h in range(2):
                    first = h * ROWS + q * 64
                    out_ref[q, r, :, h * HD : (h + 1) * HD] = whole[first : first + 64]


def attend(back, part, query, *args):
    last = part == "other"
    aliases = {}
    outs = [
        jax.ShapeDtypeStruct((4, 512, HD), jnp.float32),
        jax.ShapeDtypeStruct((4, 512, HALF), jnp.float32),
    ]
    out_specs = [vspec(), vspec()]
    if back and not last:
        aliases = {len(args) - 1: 0, len(args): 1}
    if last:
        outs = jax.ShapeDtypeStruct((4, 4, 64, 512), jnp.bfloat16)
        out_specs = vspec()
    pairs = {0: 20, 1: 32, 2: 10}[back]
    return pl.pallas_call(
        functools.partial(attend_kernel, back, part),
        out_shape=outs,
        in_specs=[vspec()] * (1 + len(args)),
        out_specs=out_specs,
        input_output_aliases=aliases,
        compiler_params=pltpu.CompilerParams(vmem_limit_bytes=24 << 20),
        cost_estimate=pl.CostEstimate(
            flops=int(pairs * 512 * 256 * 256 * 4 * 0.2),
            bytes_accessed=1 << 16,
            transcendentals=1,
        ),
        name="attend_%d_%s" % (back, part),
    )(query, *args)


def combine_kernel(got_ref, res_ref, g0_ref, g1_ref, g2_ref, g3_ref, out_ref, gain_ref):
    section = lax.axis_index("section")
    for r, ref in enumerate((g0_ref, g1_ref, g2_ref, g3_ref)):
        gain_ref[pl.ds(lax.rem(section + 4 - r, 4), 1), :] = ref[...]
    running = res_ref[...].astype(jnp.float32)
    running = [running[:, h * 512 : (h + 1) * 512] for h in range(4)]
    for layer in range(LAYERS):
        parts = [got_ref[layer * 4 + h].astype(jnp.float32) for h in range(4)]
        square = sum(jnp.sum(p * p, axis=-1, keepdims=True) for p in parts)
        norm = lax.rsqrt(square * (1.0 / (HQ * HD)) + 1e-06)
        for h in range(4):
            gain = gain_ref[layer : layer + 1, h * 512 : (h + 1) * 512]
            running[h] = running[h] + parts[h] * norm * gain
            out_ref[layer, :, h * 512 : (h + 1) * 512] = running[h].astype(jnp.bfloat16)


def per_device(queries, keys, values, segment_ids, positions, residual_in, post_gain):
    inverse = jnp.exp(-math.log(10000.0) * jnp.arange(HALF).astype(jnp.float32) / HALF)
    angle = positions.astype(jnp.float32)[:, None] * inverse[None, :]
    cosine = jnp.cos(angle)
    sine = jnp.sin(angle)
    split = jnp.stack([lax.shift_right_logical(positions, 7), positions & 127])
    places = jnp.concatenate([split, jnp.zeros((14, ROWS), jnp.int32)]).astype(jnp.bfloat16)

    def over_y(x):
        return lax.all_to_all(x, "seq", 0, 0, axis_index_groups=SHARED_Y)

    def onward(x):
        return lax.ppermute(x, "seq", NEXT_PLANE)

    def other(x):
        return lax.ppermute(x, "seq", OTHER_CORE)

    gains = [post_gain] + [
        lax.ppermute(post_gain, "section", [(i, (i + r) % 4) for i in range(4)])
        for r in (1, 2, 3)
    ]
    pieces = pl.pallas_call(
        split_v_kernel,
        out_shape=[jax.ShapeDtypeStruct((ROWS, HD), jnp.bfloat16)] * 4,
        in_specs=[vspec()],
        out_specs=[vspec()] * 4,
        name="split_v",
    )(values[0])
    pieces = [pieces[0]] + [
        lax.ppermute(pieces[i], "seq", [(d, d // 8 * 8 + (d + 2 * i) % 8) for d in range(64)])
        for i in (1, 2, 3)
    ]
    v0 = pl.pallas_call(
        order_v_kernel,
        out_shape=jax.ShapeDtypeStruct((HK, ROWS, HD), jnp.bfloat16),
        in_specs=[vspec()] * 4,
        out_specs=vspec(),
        compiler_params=pltpu.CompilerParams(vmem_limit_bytes=8 << 20),
        name="order_v",
    )(*pieces)
    k_msg = pl.pallas_call(
        rotate_k_kernel,
        out_shape=jax.ShapeDtypeStruct((HK, ROWS, HD), jnp.bfloat16),
        in_specs=[vspec()] * 3,
        out_specs=vspec(),
        name="rotate_k",
    )(cosine, sine, keys[0])
    q_msg = pl.pallas_call(
        rotate_q_kernel,
        out_shape=jax.ShapeDtypeStruct((HK, 2 * ROWS + 16, HD), jnp.bfloat16),
        in_specs=[vspec()] * 4,
        out_specs=vspec(),
        name="rotate_q",
    )(cosine, sine, places, queries[0])

    residual = lax.dynamic_slice_in_dim(residual_in, lax.axis_index("section") * 64, 64, 0)
    v1 = onward(v0)
    k0 = over_y(k_msg)
    k0, q_msg = lax.optimization_barrier((k0, q_msg))
    k1 = onward(k0)
    v1, q_msg = lax.optimization_barrier((v1, q_msg))
    query = over_y(q_msg)
    v2 = onward(v1)
    k2 = onward(k1)
    num, den = attend(0, "both", query, k0, other(k0), v0, other(v0))
    num, den, v2 = lax.optimization_barrier((num, den, v2))
    num, den = attend(1, "both", query, k1, other(k1), v1, other(v1), num, den)
    num, den, k2, residual, *gains = lax.optimization_barrier((num, den, k2, residual, *gains))
    num, den = attend(2, "own", query, k2, v2, num, den)
    sent = attend(2, "other", query, other(k2), other(v2), num, den)
    got = lax.all_to_all(
        sent.reshape(16, 64, 512), ("section", "seq"), 0, 0, axis_index_groups=SHARED_XY
    )
    back = pl.pallas_call(
        combine_kernel,
        out_shape=jax.ShapeDtypeStruct((LAYERS, 64, HQ * HD), jnp.bfloat16),
        in_specs=[vspec()] * 6,
        out_specs=vspec(),
        scratch_shapes=[VMEM((LAYERS, HQ * HD), jnp.float32)],
        compiler_params=pltpu.CompilerParams(vmem_limit_bytes=12 << 20),
        name="combine",
    )(got, residual, *gains)
    mine = lax.all_to_all(back, "section", 0, 0)
    return mine.reshape(1, ROWS, HQ * HD)


def solution(mesh):
    placed = (
        P("section", "seq", None),
        P("section", "seq", None),
        P("section", "seq", None),
        P("seq"),
        P("seq"),
        P("seq", None),
        P("section", None),
    )
    return jax.shard_map(
        per_device, mesh=mesh, in_specs=placed, out_specs=P("section", "seq", None), check_vma=False
    )
```

```python
import functools
import math

import jax
import jax.numpy as jnp
from jax import lax
from jax.experimental import pallas as pl
from jax.experimental.pallas import tpu as pltpu
from jax.sharding import PartitionSpec as P

HQ = 8
HK = 4
HD = 256
WINDOW = 4096
ROWS = 256
PLANE = 2048
LAYERS = 4
HALF = HD // 2
VMEM = pltpu.VMEM
CAP = 50.0 / math.log(2.0)

SHARED_Y = [[z * 8 + y * 2 + c for y in range(4)] for z in range(8) for c in range(2)]
SHARED_XY = [
    [x * 64 + z * 8 + y * 2 + c for x in range(4) for y in range(4)]
    for z in range(8)
    for c in range(2)
]
NEXT_PLANE = [(i, i + 8) for i in range(56)]
OTHER_CORE = [(i, i ^ 1) for i in range(64)]


def vspec():
    return pl.BlockSpec(memory_space=VMEM)


def turned(x, cosine, sine):
    first = x[:, :HALF].astype(jnp.float32)
    second = x[:, HALF:].astype(jnp.float32)
    return (
        (first * cosine - second * sine).astype(jnp.bfloat16),
        (second * cosine + first * sine).astype(jnp.bfloat16),
    )


def split_v_kernel(v_ref, *out_refs):
    y = lax.rem(lax.axis_index("seq") // 2, 4)
    for i, out_ref in enumerate(out_refs):
        lanes = pl.ds(pl.multiple_of(lax.rem(y + i, 4) * HD, HD), HD)
        out_ref[...] = v_ref[:, lanes]


def order_v_kernel(v0_ref, v1_ref, v2_ref, v3_ref, out_ref):
    y = lax.rem(lax.axis_index("seq") // 2, 4)
    for i, ref in enumerate((v0_ref, v1_ref, v2_ref, v3_ref)):
        out_ref[lax.rem(y + 4 - i, 4)] = ref[...]


def rotate_k_kernel(cos_ref, sin_ref, k_ref, km_ref):
    for h in range(HK):
        a, b = turned(k_ref[:, h * HD : (h + 1) * HD], cos_ref[...], sin_ref[...])
        km_ref[h, :, :HALF] = a
        km_ref[h, :, HALF:] = b


def rotate_q_kernel(cos_ref, sin_ref, place_ref, q_ref, qm_ref):
    for h in range(HQ):
        a, b = turned(q_ref[:, h * HD : (h + 1) * HD], cos_ref[...], sin_ref[...])
        rows = pl.ds((h % 2) * ROWS, ROWS)
        qm_ref[h // 2, rows, :HALF] = a
        qm_ref[h // 2, rows, HALF:] = b
    for h in range(HK):
        qm_ref[h, 2 * ROWS :] = place_ref[...]


def attend_kernel(back, part, q_ref, *refs):
    device = lax.axis_index("seq")
    plane0 = device // 8 * PLANE
    core = lax.rem(device, 2)
    if part == "both":
        pairs = ((refs[0], refs[2], core), (refs[1], refs[3], 1 - core))
        refs = refs[4:]
    else:
        pairs = ((refs[0], refs[1], core if part == "own" else 1 - core),)
        refs = refs[2:]
    last = part == "other"
    if back == 0:
        num, den = refs
    elif last:
        num_in, den_in, out_ref = refs
    else:
        num_in, den_in, num, den = refs
    keys0 = plane0 - back * PLANE
    for r in range(4):
        begin, end = {0: (0, r + 1), 1: (0, 4), 2: (r, 4)}[back]
        count = (end - begin) * ROWS
        query = q_ref[r, : 2 * ROWS]
        split = q_ref[r, 2 * ROWS :].astype(jnp.float32)
        place = (split[0:1] * 128.0 + split[1:2]).astype(jnp.int32)
        token = plane0 + r * 512 + core * ROWS + lax.broadcasted_iota(jnp.int32, (1, ROWS), 1)
        low = token - jnp.minimum(place, WINDOW - 1)
        low = jnp.transpose(jnp.broadcast_to(low, (HALF, ROWS)))
        low = jnp.concatenate([low, low], axis=0)
        low = jnp.concatenate([low] * (count // HALF), axis=1)
        col = lax.broadcasted_iota(jnp.int32, (1, count), 1)
        spread = col + lax.shift_right_logical(col, 8) * ROWS + begin * 512 + keys0
        total, added = None, None
        for k_ref, v_ref, side in pairs:
            score = lax.dot_general(
                query,
                k_ref[begin:end].reshape(count, HD),
                (((1,), (1,)), ((), ())),
                preferred_element_type=jnp.float32,
            )
            weight = jnp.exp2(jnp.tanh(score * (1.0 / 800.0)) * CAP)
            key = spread + side * ROWS
            ok = key >= low
            if back == 0:
                row = lax.broadcasted_iota(jnp.int32, (2 * ROWS, 1), 0) & (ROWS - 1)
                ok = ok & (key <= plane0 + r * 512 + core * ROWS + row)
            weight = jnp.where(ok, weight, 0.0)
            lanes = sum(weight[:, i * HALF : (i + 1) * HALF] for i in range(count // HALF))
            part = jnp.dot(
                weight.astype(jnp.bfloat16),
                v_ref[begin:end].reshape(count, HD),
                preferred_element_type=jnp.float32,
            )
            total = lanes if total is None else total + lanes
            added = part if added is None else added + part
        if back == 0:
            num[r] = added
            den[r] = total
        elif not last:
            num[r] = num_in[r] + added
            den[r] = den_in[r] + total
        else:
            scale = 1.0 / jnp.sum(den_in[r] + total, axis=-1, keepdims=True)
            whole = ((num_in[r] + added) * scale).astype(jnp.bfloat16)
            for q in range(4):
                for h in range(2):
                    first = h * ROWS + q * 64
                    out_ref[q, r, :, h * HD : (h + 1) * HD] = whole[first : first + 64]


def attend(back, part, query, *args):
    last = part == "other"
    aliases = {}
    outs = [
        jax.ShapeDtypeStruct((4, 512, HD), jnp.float32),
        jax.ShapeDtypeStruct((4, 512, HALF), jnp.float32),
    ]
    out_specs = [vspec(), vspec()]
    if back and not last:
        aliases = {len(args) - 1: 0, len(args): 1}
    if last:
        outs = jax.ShapeDtypeStruct((4, 4, 64, 512), jnp.bfloat16)
        out_specs = vspec()
    pairs = {0: 20, 1: 32, 2: 10}[back]
    return pl.pallas_call(
        functools.partial(attend_kernel, back, part),
        out_shape=outs,
        in_specs=[vspec()] * (1 + len(args)),
        out_specs=out_specs,
        input_output_aliases=aliases,
        compiler_params=pltpu.CompilerParams(vmem_limit_bytes=24 << 20),
        cost_estimate=pl.CostEstimate(
            flops=int(pairs * 512 * 256 * 256 * 4 * 0.2),
            bytes_accessed=1 << 16,
            transcendentals=1,
        ),
        name="attend_%d_%s" % (back, part),
    )(query, *args)


def combine_kernel(got_ref, res_ref, g0_ref, g1_ref, g2_ref, g3_ref, out_ref, gain_ref):
    section = lax.axis_index("section")
    for r, ref in enumerate((g0_ref, g1_ref, g2_ref, g3_ref)):
        gain_ref[pl.ds(lax.rem(section + 4 - r, 4), 1), :] = ref[...]
    running = res_ref[...].astype(jnp.float32)
    running = [running[:, h * 512 : (h + 1) * 512] for h in range(4)]
    for layer in range(LAYERS):
        parts = [got_ref[layer * 4 + h].astype(jnp.float32) for h in range(4)]
        square = sum(jnp.sum(p * p, axis=-1, keepdims=True) for p in parts)
        norm = lax.rsqrt(square * (1.0 / (HQ * HD)) + 1e-06)
        for h in range(4):
            gain = gain_ref[layer : layer + 1, h * 512 : (h + 1) * 512]
            running[h] = running[h] + parts[h] * norm * gain
            out_ref[layer, :, h * 512 : (h + 1) * 512] = running[h].astype(jnp.bfloat16)


def per_device(queries, keys, values, segment_ids, positions, residual_in, post_gain):
    inverse = jnp.exp(-math.log(10000.0) * jnp.arange(HALF).astype(jnp.float32) / HALF)
    angle = positions.astype(jnp.float32)[:, None] * inverse[None, :]
    cosine = jnp.cos(angle)
    sine = jnp.sin(angle)
    split = jnp.stack([lax.shift_right_logical(positions, 7), positions & 127])
    places = jnp.concatenate([split, jnp.zeros((14, ROWS), jnp.int32)]).astype(jnp.bfloat16)

    def over_y(x):
        return lax.all_to_all(x, "seq", 0, 0, axis_index_groups=SHARED_Y)

    def onward(x):
        return lax.ppermute(x, "seq", NEXT_PLANE)

    def other(x):
        return lax.ppermute(x, "seq", OTHER_CORE)

    gains = [post_gain] + [
        lax.ppermute(post_gain, "section", [(i, (i + r) % 4) for i in range(4)])
        for r in (1, 2, 3)
    ]
    pieces = pl.pallas_call(
        split_v_kernel,
        out_shape=[jax.ShapeDtypeStruct((ROWS, HD), jnp.bfloat16)] * 4,
        in_specs=[vspec()],
        out_specs=[vspec()] * 4,
        name="split_v",
    )(values[0])
    pieces = [pieces[0]] + [
        lax.ppermute(pieces[i], "seq", [(d, d // 8 * 8 + (d + 2 * i) % 8) for d in range(64)])
        for i in (1, 2, 3)
    ]
    v0 = pl.pallas_call(
        order_v_kernel,
        out_shape=jax.ShapeDtypeStruct((HK, ROWS, HD), jnp.bfloat16),
        in_specs=[vspec()] * 4,
        out_specs=vspec(),
        compiler_params=pltpu.CompilerParams(vmem_limit_bytes=8 << 20),
        name="order_v",
    )(*pieces)
    k_msg = pl.pallas_call(
        rotate_k_kernel,
        out_shape=jax.ShapeDtypeStruct((HK, ROWS, HD), jnp.bfloat16),
        in_specs=[vspec()] * 3,
        out_specs=vspec(),
        name="rotate_k",
    )(cosine, sine, keys[0])
    q_msg = pl.pallas_call(
        rotate_q_kernel,
        out_shape=jax.ShapeDtypeStruct((HK, 2 * ROWS + 16, HD), jnp.bfloat16),
        in_specs=[vspec()] * 4,
        out_specs=vspec(),
        name="rotate_q",
    )(cosine, sine, places, queries[0])

    residual = lax.dynamic_slice_in_dim(residual_in, lax.axis_index("section") * 64, 64, 0)
    v1 = onward(v0)
    k0 = over_y(k_msg)
    k0, q_msg = lax.optimization_barrier((k0, q_msg))
    k1 = onward(k0)
    v1, q_msg = lax.optimization_barrier((v1, q_msg))
    query = over_y(q_msg)
    v2 = onward(v1)
    k2 = onward(k1)
    num, den = attend(0, "both", query, k0, other(k0), v0, other(v0))
    num, den, v2 = lax.optimization_barrier((num, den, v2))
    num, den = attend(1, "both", query, k1, other(k1), v1, other(v1), num, den)
    num, den, k2, residual = lax.optimization_barrier((num, den, k2, residual))
    num, den = attend(2, "own", query, k2, v2, num, den)
    sent = attend(2, "other", query, other(k2), other(v2), num, den)
    got = lax.all_to_all(
        sent.reshape(16, 64, 512), ("section", "seq"), 0, 0, axis_index_groups=SHARED_XY
    )
    back = pl.pallas_call(
        combine_kernel,
        out_shape=jax.ShapeDtypeStruct((LAYERS, 64, HQ * HD), jnp.bfloat16),
        in_specs=[vspec()] * 6,
        out_specs=vspec(),
        scratch_shapes=[VMEM((LAYERS, HQ * HD), jnp.float32)],
        compiler_params=pltpu.CompilerParams(vmem_limit_bytes=12 << 20),
        name="combine",
    )(got, residual, *gains)
    mine = lax.all_to_all(back, "section", 0, 0)
    return mine.reshape(1, ROWS, HQ * HD)


def solution(mesh):
    placed = (
        P("section", "seq", None),
        P("section", "seq", None),
        P("section", "seq", None),
        P("seq"),
        P("seq"),
        P("seq", None),
        P("section", None),
    )
    return jax.shard_map(
        per_device, mesh=mesh, in_specs=placed, out_specs=P("section", "seq", None), check_vma=False
    )
```
